512 devices in a mesh: snap: 16 (over y, x), plane: 32 (over z, core).
Axes of the slice: x: 4, y: 4, z: 16, core: 2. Of those that a mesh axis runs over, the one named last changes fastest.
Arguments:
- velocity: bfloat16 [16, 128, 3, 128, 128], P('snap', 'plane'), may hold values from -6 to 6
- plane_count: int32 [32], P('plane'), may hold values from 1 to 4, as said below
- inv_span: float32 [32, 4], P('plane'), may hold values from 0.5 to 4
- kernels: float32 [3, 2, 3, 3], replicated, may hold values from -2.4 to 2.4
- omega_block: int32 [32, 4], P('plane'), may hold values from 0 to 7
- omega_table: bfloat16 [8, 9, 32, 256], replicated, may hold values from -0.0625 to 0.0625
- omega_stream: bfloat16 [32, 256], replicated, may hold values from -6 to 6
- wall_shear: bfloat16 [16, 2, 128, 128], P('snap', None, 'plane'), may hold values from -6 to 6
Outputs:
- sketch: float32 [2, 32, 32, 256], P(None, 'plane', 'snap')
- gram: float32 [256, 256], replicated
The draws below stay inside these ranges and needn't reach their ends.
Inputs may be any that keep to these rules, and one draw needn't show every extreme that they name: `plane_count`: every index of plane holds 1 or more live slots, slots 0 onwards; some index holds 4.
All inputs are finite; a program needn't handle non-finite values.
Results may differ from the reference program's by a relative error of at most 0.0043.
Values may be sent and summed in bfloat16 or wider, within the bound.
No kernel may reach another device: no remote copies, remote signals or barrier semaphores. Data moves between devices by JAX's collectives and lax.ppermute only.
A program may use at most 64 MiB of HBM per device.

```python
import math
import jax
import jax.numpy as jnp
from jax import lax

X = 128
ZW = 128
CAP = 4
CH = 9
K = 256
BLOCKS = 8
SNAPS = 16
SLOTS = 128
ZF = 32
XF = 32
N_PLANE = 32


def draw_plane_count(key, part):
    counts = jax.random.randint(key, (N_PLANE,), 1, CAP + 1)
    chosen = jax.random.randint(jax.random.fold_in(key, 7), (), 0, N_PLANE)
    return jnp.where(jnp.arange(N_PLANE) == chosen, CAP, counts).astype(jnp.int32)


def with_ends(drawn, key, low, high):
    index_at = [jax.random.randint(jax.random.fold_in(key, axis), (), 0, length) for axis, length in enumerate(drawn.shape)]
    longest = drawn.shape.index(max(drawn.shape))
    beside = index_at[:longest] + [(index_at[longest] + 1) % drawn.shape[longest]] + index_at[longest + 1:]
    return drawn.at[tuple(index_at)].set(low).at[tuple(beside)].set(high)


def block_levels(key, dims, cuts, least, top_value):
    factor_of = 1.0
    for axis_at, parts in cuts:
        steps = jax.random.uniform(jax.random.fold_in(jax.random.fold_in(key, 6), axis_at), (parts,), jnp.float32, least / len(cuts), top_value / len(cuts))
        factor_of = factor_of * jnp.repeat(jnp.exp(steps), dims[axis_at] // parts).reshape((-1,) + (1,) * (len(dims) - 1 - axis_at))
    return factor_of


def scatter_about(key, extent, width, most, pieces=(), kind=jnp.bfloat16):
    values = jax.random.normal(key, extent, jnp.float32) * width
    if len(pieces) > 0:
        values = block_levels(key, extent, pieces, -0.22, 0.18) * values
    return jnp.clip(values, min=-most, max=most).astype(kind)


def setup_inputs(seed: int = 0) -> dict:
    arg_keys = jax.random.split(jax.random.key(seed), 9)
    velocity = scatter_about(arg_keys[0], (SNAPS, SLOTS, 3, ZW, X), 1.0, 6.0, ((0, 16), (1, 32)))
    plane_count = draw_plane_count(jax.random.fold_in(arg_keys[8], 71), 0)
    inv_span = jnp.clip(jnp.exp(math.log(4.0) - 2.0794415 * jax.random.uniform(arg_keys[2], (N_PLANE, CAP), jnp.float32) ** block_levels(arg_keys[2], (N_PLANE, CAP), ((0, 32),), -0.2, 0.2)), 0.5, 4.0)
    kernels = scatter_about(arg_keys[3], (3, 2, 3, 3), 0.4, 2.4, (), jnp.float32)
    omega_block = with_ends(jax.random.randint(arg_keys[4], (N_PLANE, CAP), 0, BLOCKS), jax.random.fold_in(arg_keys[4], 1), 0, BLOCKS - 1).astype(jnp.int32)
    omega_table = scatter_about(arg_keys[5], (BLOCKS, CH, ZF, K), (CH * ZF * XF) ** -0.5, 0.0625)
    omega_stream = scatter_about(arg_keys[6], (XF, K), 1.0, 6.0)
    wall_shear = scatter_about(arg_keys[7], (SNAPS, 2, ZW, X), 1.0, 6.0, ((0, 16), (2, 32)))
    return {"velocity": velocity, "plane_count": plane_count, "inv_span": inv_span, "kernels": kernels, "omega_block": omega_block, "omega_table": omega_table, "omega_stream": omega_stream, "wall_shear": wall_shear}


def features(centre, below, above, span, kernels):
    snaps, comps, zw, xw = centre.shape
    field = centre.astype(jnp.float32)
    padded = jnp.pad(field, ((0, 0), (0, 0), (1, 1), (1, 1)))
    first = jnp.zeros_like(field)
    second = jnp.zeros_like(field)
    for row_a in range(3):
        for col_b in range(3):
            window = padded[:, :, row_a:row_a + zw, col_b:col_b + xw]
            first = first + kernels[:, 0, row_a, col_b][None, :, None, None] * window
            second = second + kernels[:, 1, row_a, col_b][None, :, None, None] * window
    normal = (above.astype(jnp.float32) - below.astype(jnp.float32)) * span
    grads = jnp.stack([first, second, normal], axis=2).reshape(snaps, 9, zw, xw)
    filtered = grads.reshape(snaps, 9, zw // 4, 4, xw // 4, 4).mean(axis=(3, 5))
    return filtered.astype(jnp.bfloat16)


def reference(velocity, plane_count, inv_span, kernels, omega_block, omega_table, omega_stream, wall_shear):
    npl = plane_count.shape[0]
    cap = inv_span.shape[1]
    counts = plane_count.astype(jnp.int32)
    spans = inv_span.reshape(-1)
    blocks = omega_block.reshape(-1).astype(jnp.int32)

    def slot_term(index):
        owner = index // cap
        slot = index % cap
        live = slot < counts[owner]
        has_up = (slot + 1 < counts[owner]) | (owner + 1 < npl)
        up_index = jnp.where(slot + 1 < counts[owner], index + 1, (owner + 1) * cap)
        prev_owner = jnp.maximum(owner - 1, 0)
        has_down = (slot >= 1) | (owner >= 1)
        down_index = jnp.where(slot >= 1, index - 1, prev_owner * cap + counts[prev_owner] - 1)
        up_index = jnp.clip(up_index, 0, npl * cap - 1).astype(jnp.int32)
        down_index = jnp.clip(down_index, 0, npl * cap - 1).astype(jnp.int32)
        centre = lax.dynamic_index_in_dim(velocity, index.astype(jnp.int32), 1, keepdims=False)
        above = lax.dynamic_index_in_dim(velocity, up_index, 1, keepdims=False)
        below = lax.dynamic_index_in_dim(velocity, down_index, 1, keepdims=False)
        above = jnp.where(has_up, above, jnp.zeros_like(above))
        below = jnp.where(has_down, below, jnp.zeros_like(below))
        feats = features(centre, below, above, spans[index], kernels)
        proj = jnp.einsum('sczx,xk->sczk', feats, omega_stream, preferred_element_type=jnp.float32)
        table = lax.dynamic_index_in_dim(omega_table, blocks[index], 0, keepdims=False).astype(jnp.float32)
        term = jnp.einsum('sczk,czk->sk', proj, table, precision=lax.Precision.HIGHEST)
        return jnp.where(live, term, jnp.zeros_like(term))

    terms = lax.map(slot_term, jnp.arange(npl * cap, dtype=jnp.int32))
    coef = jnp.sum(terms, axis=0)
    snaps, comps, zw, xw = wall_shear.shape
    shear_f = wall_shear.astype(jnp.float32).reshape(snaps, comps, zw // 4, 4, xw // 4, 4).mean(axis=(3, 5))
    sketch = jnp.einsum('smzx,sk->mzxk', shear_f, coef, precision=lax.Precision.HIGHEST)
    flat = sketch.reshape(-1, sketch.shape[-1])
    gram = jnp.dot(flat.T, flat, precision=lax.Precision.HIGHEST) / jnp.float32(flat.shape[0])
    return sketch, gram
```

```python
import jax
import jax.numpy as jnp
from jax import lax
from jax.experimental import pallas as pl
from jax.experimental.pallas import tpu as pltpu
from jax.sharding import Mesh, PartitionSpec as P

CAP = 4
ROWS = 1536
PAD = 8
SMALL = 1.0 / 16.0
HI = lax.Precision.HIGHEST


def iota(shape, dim):
    return lax.broadcasted_iota(jnp.int32, shape, dim)


def split(value):
    high = value.astype(jnp.bfloat16)
    low = (value - high.astype(jnp.float32)).astype(jnp.bfloat16)
    return high, low


def project_kernel(own, inner, outer, vel_hbm, table_hbm, stream, shear, out, vel, table, pooled, vsem, tsem):
    copies = []
    for c in range(CAP):
        part = pl.ds(c * 384, 384)
        copy = pltpu.make_async_copy(vel_hbm.at[part], vel.at[part], vsem.at[c])
        copy.start()
        copies.append(copy)
    table_copy = pltpu.make_async_copy(table_hbm, table, tsem)
    table_copy.start()

    count = own[8].astype(jnp.int32)
    odd = own[9] > 0.5
    far = own[10] > 0.5

    def pick(low, high):
        return jnp.where(odd, low, high)

    spans = [own[c] for c in range(CAP)]
    blocks = [own[4 + c].astype(jnp.int32) for c in range(CAP)]
    prev_last = jnp.maximum(pick(inner[8], outer[8]).astype(jnp.int32) - 1, 0)
    prev_span = pick(inner[prev_last], outer[prev_last])
    prev_block = pick(inner[4 + prev_last], outer[4 + prev_last]).astype(jnp.int32)
    next_span = pick(outer[0], inner[0])
    next_block = pick(outer[4], inner[4]).astype(jnp.int32)

    lane = iota((128, 128), 1)
    gap = iota((128, 128), 0) - 4 * (lane % 32) - lane // 32 + 1
    pool = jnp.where((gap >= 0) & (gap < 4) & (lane < 96), 1.0, 0.0).astype(jnp.bfloat16)

    group = iota((8, 128), 1) // 32

    def tap(i, q, a):
        at = 64 + ((i * 2 + q) * 3 + a) * 3
        picked = jnp.where(group == 0, own[at], jnp.where(group == 1, own[at + 1], own[at + 2]))
        return jnp.where(group < 3, picked * SMALL, 0.0)

    taps = {(i, q, a): tap(i, q, a) for i in range(3) for q in range(2) for a in range(3)}
    zeros = jnp.zeros((32, 256), jnp.bfloat16)
    omega = stream[...]
    spread = jnp.concatenate([omega, zeros, zeros, zeros], axis=0)
    centre = jnp.concatenate([zeros, omega, zeros, zeros] * 2, axis=0)
    first_row = iota((32, 128), 0) == 0
    last_row = iota((32, 128), 0) == 31

    planes, normals = [], []
    for c in range(CAP):
        copies[c].wait()
        pooled[pl.ds(PAD + c * 384, 384), :] = jnp.dot(
            vel[pl.ds(c * 384, 384), :], pool, preferred_element_type=jnp.float32
        )
    for c in range(CAP):
        feats, centres = [], []
        for i in range(3):
            base = PAD + (c * 3 + i) * 128
            row = [pooled[pl.ds(base + j, 32, stride=4), :] for j in range(4)]
            before = jnp.where(first_row, 0.0, pooled[pl.ds(base - 1, 32, stride=4), :])
            after = jnp.where(last_row, 0.0, pooled[pl.ds(base + 4, 32, stride=4), :])
            inside = row[1] + row[2]
            head = row[0] + inside
            window = (before + head, head + row[3], inside + row[3] + after)
            for q in range(2):
                mixed = sum(
                    (window[a].reshape(4, 8, 128) * taps[i, q, a][None]).reshape(32, 128) for a in range(3)
                )
                folded = mixed + pltpu.roll(mixed, 96, 1) + pltpu.roll(mixed, 64, 1)
                feats.append(folded.astype(jnp.bfloat16))
            centres.append(jnp.concatenate(split(window[1] * SMALL), axis=1))
        planes.append(
            jnp.dot(jnp.concatenate(feats, axis=0), spread, preferred_element_type=jnp.float32)
        )
        normals.append(
            jnp.dot(jnp.concatenate(centres, axis=0), centre, preferred_element_type=jnp.float32)
        )

    table_copy.wait()
    total = jnp.zeros((8, 256), jnp.float32)

    def rows_of(block, channel):
        return table[block, channel * 32 : channel * 32 + 32, :].astype(jnp.float32)

    for c in range(CAP):
        live = c < count
        alive = jnp.where(live, 1.0, 0.0)
        up_span = spans[c - 1] if c else prev_span
        up_block = blocks[c - 1] if c else prev_block
        if c + 1 < CAP:
            more = c + 1 < count
            down_span = jnp.where(more, spans[c + 1], next_span)
            down_block = jnp.where(more, blocks[c + 1], next_block)
        else:
            down_span, down_block = next_span, next_block
        part = jnp.zeros((8, 256), jnp.float32)
        for i in range(3):
            for q in range(2):
                at = (i * 2 + q) * 32
                part += (planes[c][at : at + 32] * rows_of(blocks[c], 3 * i + q)).reshape(4, 8, 256).sum(0)
            weight = up_span * rows_of(up_block, 3 * i + 2) - down_span * rows_of(down_block, 3 * i + 2)
            part += (normals[c][i * 32 : i * 32 + 32] * weight).reshape(4, 8, 256).sum(0)
        total += alive * part

    coef = jnp.sum(total, axis=0, keepdims=True)
    shear_pooled = jnp.dot(shear[...], pool, preferred_element_type=jnp.float32) * SMALL
    first = jnp.sum(shear_pooled[0:4], axis=0, keepdims=True)
    second = jnp.sum(shear_pooled[4:8], axis=0, keepdims=True)
    first = jnp.broadcast_to(first, (8, 128))
    second = jnp.broadcast_to(second, (8, 128))
    low = jnp.where(group == 0, pltpu.roll(first, 96, 1), jnp.where(group == 1, second, 0.0))
    wall = jnp.where(far, pltpu.roll(low, 64, 1), low)
    at_row = iota((8, 128), 0)
    tile = jnp.where(
        at_row == 0,
        jnp.broadcast_to(coef[:, :128], (8, 128)),
        jnp.where(at_row == 1, jnp.broadcast_to(coef[:, 128:], (8, 128)), jnp.where(at_row == 2, wall, 0.0)),
    )
    for copy_at in range(out.shape[0]):
        out[copy_at] = tile


def project(own, inner, outer, velocity, table, stream, shear, copies):
    smem = pl.BlockSpec(memory_space=pltpu.SMEM)
    vmem = pl.BlockSpec(memory_space=pltpu.VMEM)
    hbm = pl.BlockSpec(memory_space=pl.ANY)
    return pl.pallas_call(
        project_kernel,
        out_shape=jax.ShapeDtypeStruct((copies, 8, 128), jnp.float32),
        in_specs=[smem, smem, smem, hbm, hbm, vmem, vmem],
        out_specs=vmem,
        scratch_shapes=[
            pltpu.VMEM((ROWS, 128), jnp.bfloat16),
            pltpu.VMEM((8, 288, 256), jnp.bfloat16),
            pltpu.VMEM((ROWS + 2 * PAD, 128), jnp.float32),
            pltpu.SemaphoreType.DMA((CAP,)),
            pltpu.SemaphoreType.DMA,
        ],
        name="project",
    )(own, inner, outer, velocity, table, stream, shear)


def merge_kernel(rows, out):
    low = jnp.sum(rows[pl.ds(0, 16, stride=8), :], axis=0, keepdims=True)
    high = jnp.sum(rows[pl.ds(1, 16, stride=8), :], axis=0, keepdims=True)
    wall = rows[pl.ds(2, 8, stride=16), :] + rows[pl.ds(10, 8, stride=16), :]
    at_row = iota((8, 128), 0)
    coef = jnp.where(at_row == 0, low, jnp.where(at_row == 1, high, 0.0))
    tile = jnp.concatenate([wall, coef], axis=0)
    for copy_at in range(out.shape[0]):
        out[copy_at] = tile


def merge(rows, copies):
    return pl.pallas_call(
        merge_kernel,
        out_shape=jax.ShapeDtypeStruct((copies, 16, 128), jnp.float32),
        in_specs=[pl.BlockSpec(memory_space=pltpu.VMEM)],
        out_specs=pl.BlockSpec(memory_space=pltpu.VMEM),
        name="merge",
    )(rows)


def finish_kernel(place, rows, sketch, gram, full):
    def across(at):
        return rows[pl.ds(at, 16, stride=32), :]

    coef = jnp.concatenate([across(8) + across(24), across(9) + across(25)], axis=1)
    wall = jnp.concatenate([across(16 * core + r) for core in range(2) for r in range(8)], axis=1)
    inner = lax.dot_general(wall, wall, (((1,), (1,)), ((), ())), precision=HI, preferred_element_type=jnp.float32)
    right = jnp.dot(inner, coef, precision=HI, preferred_element_type=jnp.float32) * (1.0 / 2048.0)
    outer = (((0,), (0,)), ((), ()))
    gram[...] = lax.dot_general(coef, right, outer, precision=HI, preferred_element_type=jnp.float32)
    mine = across(place[0])
    full[...] = lax.dot_general(mine, coef, outer, precision=HI, preferred_element_type=jnp.float32)
    for m in range(2):
        for x in range(2):
            sketch[m, 0, x : x + 1, :] = full[pl.ds(place[1] + 32 * m + x, 1), :]


def finish(place, rows):
    vmem = pl.BlockSpec(memory_space=pltpu.VMEM)
    return pl.pallas_call(
        finish_kernel,
        out_shape=(
            jax.ShapeDtypeStruct((2, 1, 2, 256), jnp.float32),
            jax.ShapeDtypeStruct((256, 256), jnp.float32),
        ),
        in_specs=[pl.BlockSpec(memory_space=pltpu.SMEM), vmem],
        out_specs=(vmem, vmem),
        scratch_shapes=[pltpu.VMEM((128, 256), jnp.float32)],
        name="finish",
    )(place, rows)


def per_device(velocity, plane_count, inv_span, kernels, omega_block, omega_table, omega_stream, wall_shear):
    planes = lax.axis_size(("z", "core"))
    chips, snaps = lax.axis_size("z"), lax.axis_size("snap")
    snap, z, core = lax.axis_index("snap"), lax.axis_index("z"), lax.axis_index("core")
    flags = jnp.stack([plane_count[0], core, z % 2]).astype(jnp.float32)
    own = jnp.concatenate(
        [
            inv_span.reshape(-1),
            omega_block.reshape(-1).astype(jnp.float32),
            flags,
            jnp.zeros((53,), jnp.float32),
            kernels.reshape(-1),
            jnp.zeros((10,), jnp.float32),
        ]
    )
    inner = lax.ppermute(own, ("z", "core"), [(p, p ^ 1) for p in range(planes)])
    outer = lax.ppermute(
        own, ("z", "core"), [(p, p + 1 if p % 2 else p - 1) for p in range(1, planes - 1)]
    )
    sent = project(
        own,
        inner,
        outer,
        velocity.reshape(ROWS, 128),
        omega_table.reshape(8, 288, 256),
        omega_stream,
        wall_shear.reshape(8, 128),
        chips,
    )
    got = lax.all_to_all(sent, "z", 0, 0, tiled=True)
    sent = merge(got.reshape(chips * 8, 128), snaps * 2)
    got = lax.all_to_all(sent, ("snap", "core"), 0, 0, tiled=True)
    place = jnp.stack([16 * core + z // 2, (z % 2) * 64 + 2 * snap]).astype(jnp.int32)
    return finish(place, got.reshape(snaps * 2 * 16, 128))


def solution(mesh):
    chips = mesh.shape["plane"] // 2
    fine = Mesh(mesh.devices.reshape(mesh.shape["snap"], chips, 2), ("snap", "z", "core"))
    plane = ("z", "core")
    return jax.shard_map(
        per_device,
        mesh=fine,
        in_specs=(
            P("snap", plane, None, None, None),
            P(plane),
            P(plane, None),
            P(),
            P(plane, None),
            P(),
            P(),
            P("snap", None, plane, None),
        ),
        out_specs=(P(None, plane, "snap", None), P()),
        check_vma=False,
    )
```

```python
import jax
import jax.numpy as jnp
from jax import lax
from jax.experimental import pallas as pl
from jax.experimental.pallas import tpu as pltpu
from jax.sharding import Mesh, PartitionSpec as P

CAP = 4
ROWS = 1536
PAD = 8
SMALL = 1.0 / 16.0
HI = lax.Precision.HIGHEST
LONG = pl.CostEstimate(flops=10**10, bytes_accessed=10**7, transcendentals=0)
GRANT = pltpu.CompilerParams(vmem_limit_bytes=8 << 20)


def iota(shape, dim):
    return lax.broadcasted_iota(jnp.int32, shape, dim)


def split(value):
    high = value.astype(jnp.bfloat16)
    low = (value - high.astype(jnp.float32)).astype(jnp.bfloat16)
    return high, low


def blank_kernel(out):
    out[...] = jnp.zeros((1, 128), jnp.float32)


def blank():
    return pl.pallas_call(
        blank_kernel,
        out_shape=jax.ShapeDtypeStruct((1, 128), jnp.float32),
        out_specs=pl.BlockSpec(memory_space=pltpu.VMEM),
        compiler_params=GRANT,
        cost_estimate=LONG,
        name="blank",
    )()


def pack_kernel(count, base, spans, blocks, out):
    at = iota((1, 128), 1)
    out[...] = base[...] + jnp.where(at == 8, count[0].astype(jnp.float32), 0.0)
    out[0:1, 0:CAP] = spans[...]
    out[0:1, CAP : 2 * CAP] = blocks[...].astype(jnp.float32)


def pack(count, spans, blocks):
    vmem = pl.BlockSpec(memory_space=pltpu.VMEM)
    return pl.pallas_call(
        pack_kernel,
        out_shape=jax.ShapeDtypeStruct((1, 128), jnp.float32),
        in_specs=[pl.BlockSpec(memory_space=pltpu.SMEM), vmem, vmem, vmem],
        out_specs=vmem,
        compiler_params=GRANT,
        cost_estimate=LONG,
        name="pack",
    )(count, blank(), spans, blocks).reshape(128)


def project_kernel(place, own, inner, outer, taps_in, vel, table, stream, shear, out, pooled):
    count = own[8].astype(jnp.int32)
    odd = place[0] == 1
    far = place[1] % 2 == 1

    def pick(low, high):
        return jnp.where(odd, low, high)

    spans = [own[c] for c in range(CAP)]
    blocks = [own[4 + c].astype(jnp.int32) for c in range(CAP)]
    prev_last = jnp.maximum(pick(inner[8], outer[8]).astype(jnp.int32) - 1, 0)
    prev_span = pick(inner[prev_last], outer[prev_last])
    prev_block = pick(inner[4 + prev_last], outer[4 + prev_last]).astype(jnp.int32)
    next_span = pick(outer[0], inner[0])
    next_block = pick(outer[4], inner[4]).astype(jnp.int32)

    lane = iota((128, 128), 1)
    gap = iota((128, 128), 0) - 4 * (lane % 32) - lane // 32 + 1
    pool = jnp.where((gap >= 0) & (gap < 4) & (lane < 96), 1.0, 0.0).astype(jnp.bfloat16)

    group = iota((8, 128), 1) // 32

    def tap(i, q, a):
        at = ((i * 2 + q) * 3 + a) * 3
        picked = jnp.where(group == 0, taps_in[at], jnp.where(group == 1, taps_in[at + 1], taps_in[at + 2]))
        return jnp.where(group < 3, picked * SMALL, 0.0)

    taps = {(i, q, a): tap(i, q, a) for i in range(3) for q in range(2) for a in range(3)}
    zeros = jnp.zeros((32, 256), jnp.bfloat16)
    omega = stream[...]
    spread = jnp.concatenate([omega, zeros, zeros, zeros], axis=0)
    centre = jnp.concatenate([zeros, omega, zeros, zeros] * 2, axis=0)
    first_row = iota((32, 128), 0) == 0
    last_row = iota((32, 128), 0) == 31

    planes, normals = [], []
    for c in range(CAP):
        pooled[pl.ds(PAD + c * 384, 384), :] = jnp.dot(
            vel[pl.ds(c * 384, 384), :], pool, preferred_element_type=jnp.float32
        )
    for c in range(CAP):
        feats, centres = [], []
        for i in range(3):
            base = PAD + (c * 3 + i) * 128
            row = [pooled[pl.ds(base + j, 32, stride=4), :] for j in range(4)]
            before = jnp.where(first_row, 0.0, pooled[pl.ds(base - 1, 32, stride=4), :])
            after = jnp.where(last_row, 0.0, pooled[pl.ds(base + 4, 32, stride=4), :])
            inside = row[1] + row[2]
            head = row[0] + inside
            window = (before + head, head + row[3], inside + row[3] + after)
            for q in range(2):
                mixed = sum(
                    (window[a].reshape(4, 8, 128) * taps[i, q, a][None]).reshape(32, 128) for a in range(3)
                )
                folded = mixed + pltpu.roll(mixed, 96, 1) + pltpu.roll(mixed, 64, 1)
                feats.append(folded.astype(jnp.bfloat16))
            centres.append(jnp.concatenate(split(window[1] * SMALL), axis=1))
        planes.append(
            jnp.dot(jnp.concatenate(feats, axis=0), spread, preferred_element_type=jnp.float32)
        )
        normals.append(
            jnp.dot(jnp.concatenate(centres, axis=0), centre, preferred_element_type=jnp.float32)
        )

    total = jnp.zeros((8, 256), jnp.float32)

    def rows_of(block, channel):
        return table[block, channel * 32 : channel * 32 + 32, :].astype(jnp.float32)

    for c in range(CAP):
        live = c < count
        alive = jnp.where(live, 1.0, 0.0)
        up_span = spans[c - 1] if c else prev_span
        up_block = blocks[c - 1] if c else prev_block
        if c + 1 < CAP:
            more = c + 1 < count
            down_span = jnp.where(more, spans[c + 1], next_span)
            down_block = jnp.where(more, blocks[c + 1], next_block)
        else:
            down_span, down_block = next_span, next_block
        part = jnp.zeros((8, 256), jnp.float32)
        for i in range(3):
            for q in range(2):
                at = (i * 2 + q) * 32
                part += (planes[c][at : at + 32] * rows_of(blocks[c], 3 * i + q)).reshape(4, 8, 256).sum(0)
            weight = up_span * rows_of(up_block, 3 * i + 2) - down_span * rows_of(down_block, 3 * i + 2)
            part += (normals[c][i * 32 : i * 32 + 32] * weight).reshape(4, 8, 256).sum(0)
        total += alive * part

    coef = jnp.sum(total, axis=0, keepdims=True)
    shear_pooled = jnp.dot(shear[...], pool, preferred_element_type=jnp.float32) * SMALL
    first = jnp.sum(shear_pooled[0:4], axis=0, keepdims=True)
    second = jnp.sum(shear_pooled[4:8], axis=0, keepdims=True)
    first = jnp.broadcast_to(first, (8, 128))
    second = jnp.broadcast_to(second, (8, 128))
    low = jnp.where(group == 0, pltpu.roll(first, 96, 1), jnp.where(group == 1, second, 0.0))
    wall = jnp.where(far, pltpu.roll(low, 64, 1), low)
    at_row = iota((8, 128), 0)
    tile = jnp.where(
        at_row == 0,
        jnp.broadcast_to(coef[:, :128], (8, 128)),
        jnp.where(at_row == 1, jnp.broadcast_to(coef[:, 128:], (8, 128)), jnp.where(at_row == 2, wall, 0.0)),
    )
    for copy_at in range(out.shape[0]):
        out[copy_at] = tile


def project(place, own, inner, outer, taps, velocity, table, stream, shear, copies):
    smem = pl.BlockSpec(memory_space=pltpu.SMEM)
    vmem = pl.BlockSpec(memory_space=pltpu.VMEM)
    return pl.pallas_call(
        project_kernel,
        out_shape=jax.ShapeDtypeStruct((copies, 8, 128), jnp.float32),
        in_specs=[smem, smem, smem, smem, smem, vmem, vmem, vmem, vmem],
        out_specs=vmem,
        scratch_shapes=[
            pltpu.VMEM((ROWS + 2 * PAD, 128), jnp.float32),
        ],
        compiler_params=GRANT,
        name="project",
    )(place, own, inner, outer, taps, velocity, table, stream, shear)


def merge_kernel(rows, out):
    low = jnp.sum(rows[pl.ds(0, 16, stride=8), :], axis=0, keepdims=True)
    high = jnp.sum(rows[pl.ds(1, 16, stride=8), :], axis=0, keepdims=True)
    wall = rows[pl.ds(2, 8, stride=16), :] + rows[pl.ds(10, 8, stride=16), :]
    at_row = iota((8, 128), 0)
    coef = jnp.where(at_row == 0, low, jnp.where(at_row == 1, high, 0.0))
    tile = jnp.concatenate([wall, coef], axis=0)
    for copy_at in range(out.shape[0]):
        out[copy_at] = tile


def merge(rows, copies):
    return pl.pallas_call(
        merge_kernel,
        out_shape=jax.ShapeDtypeStruct((copies, 16, 128), jnp.float32),
        in_specs=[pl.BlockSpec(memory_space=pltpu.VMEM)],
        out_specs=pl.BlockSpec(memory_space=pltpu.VMEM),
        compiler_params=GRANT,
        name="merge",
    )(rows)


def finish_kernel(place, rows, sketch, gram, full):
    def across(at):
        return rows[pl.ds(at, 16, stride=32), :]

    coef = jnp.concatenate([across(8) + across(24), across(9) + across(25)], axis=1)
    wall = jnp.concatenate([across(16 * core + r) for core in range(2) for r in range(8)], axis=1)
    inner = lax.dot_general(wall, wall, (((1,), (1,)), ((), ())), precision=HI, preferred_element_type=jnp.float32)
    right = jnp.dot(inner, coef, precision=HI, preferred_element_type=jnp.float32) * (1.0 / 2048.0)
    outer = (((0,), (0,)), ((), ()))
    gram[...] = lax.dot_general(coef, right, outer, precision=HI, preferred_element_type=jnp.float32)
    core, chip, snap = place[0], place[1], place[2]
    mine = across(16 * core + chip // 2)
    base = (chip % 2) * 64 + 2 * snap
    full[...] = lax.dot_general(mine, coef, outer, precision=HI, preferred_element_type=jnp.float32)
    for m in range(2):
        for x in range(2):
            sketch[m, 0, x : x + 1, :] = full[pl.ds(base + 32 * m + x, 1), :]


def finish(place, rows):
    vmem = pl.BlockSpec(memory_space=pltpu.VMEM)
    return pl.pallas_call(
        finish_kernel,
        out_shape=(
            jax.ShapeDtypeStruct((2, 1, 2, 256), jnp.float32),
            jax.ShapeDtypeStruct((256, 256), jnp.float32),
        ),
        in_specs=[pl.BlockSpec(memory_space=pltpu.SMEM), vmem],
        out_specs=(vmem, vmem),
        scratch_shapes=[pltpu.VMEM((128, 256), jnp.float32)],
        compiler_params=GRANT,
        name="finish",
    )(place, rows)


def per_device(velocity, plane_count, inv_span, kernels, omega_block, omega_table, omega_stream, wall_shear):
    planes = lax.axis_size(("z", "core"))
    chips, snaps = lax.axis_size("z"), lax.axis_size("snap")
    snap, z, core = lax.axis_index("snap"), lax.axis_index("z"), lax.axis_index("core")
    own = pack(plane_count, inv_span, omega_block)
    inner = lax.ppermute(own, ("z", "core"), [(p, p ^ 1) for p in range(planes)])
    outer = lax.ppermute(
        own, ("z", "core"), [(p, p + 1 if p % 2 else p - 1) for p in range(1, planes - 1)]
    )
    place = jnp.stack([core, z, snap]).astype(jnp.int32)
    sent = project(
        place,
        own,
        inner,
        outer,
        kernels.reshape(-1),
        velocity.reshape(ROWS, 128),
        omega_table.reshape(8, 288, 256),
        omega_stream,
        wall_shear.reshape(8, 128),
        chips,
    )
    got = lax.all_to_all(sent, "z", 0, 0, tiled=True)
    sent = merge(got.reshape(chips * 8, 128), snaps * 2)
    got = lax.all_to_all(sent, ("snap", "core"), 0, 0, tiled=True)
    return finish(place, got.reshape(snaps * 2 * 16, 128))


def solution(mesh):
    chips = mesh.shape["plane"] // 2
    fine = Mesh(mesh.devices.reshape(mesh.shape["snap"], chips, 2), ("snap", "z", "core"))
    plane = ("z", "core")
    return jax.shard_map(
        per_device,
        mesh=fine,
        in_specs=(
            P("snap", plane, None, None, None),
            P(plane),
            P(plane, None),
            P(),
            P(plane, None),
            P(),
            P(),
            P("snap", None, plane, None),
        ),
        out_specs=(P(None, plane, "snap", None), P()),
        check_vma=False,
    )
```

```python
import jax
import jax.numpy as jnp
from jax import lax
from jax.experimental import pallas as pl
from jax.experimental.pallas import tpu as pltpu
from jax.sharding import Mesh, PartitionSpec as P

CAP = 4
BLOCKS = 8
ROWS = 1536
PAD = 8
SENT = 24
SMALL = 1.0 / 16.0
LONG = pl.CostEstimate(flops=10**10, bytes_accessed=10**7, transcendentals=0)
GRANT = pltpu.CompilerParams(vmem_limit_bytes=8 << 20)
SMEM = pl.BlockSpec(memory_space=pltpu.SMEM)
VMEM = pl.BlockSpec(memory_space=pltpu.VMEM)
OVER_ROWS = (((0,), (0,)), ((), ()))


def iota(shape, dim):
    return lax.broadcasted_iota(jnp.int32, shape, dim)


def split(value):
    high = value.astype(jnp.bfloat16)
    low = (value - high.astype(jnp.float32)).astype(jnp.bfloat16)
    return high, low


def dot(left, right):
    return jnp.dot(left, right, preferred_element_type=jnp.float32)


def call(kernel, name, out, ins, scratch=(), cost=None):
    return pl.pallas_call(
        kernel,
        out_shape=out,
        in_specs=ins,
        out_specs=jax.tree.map(lambda _: VMEM, out),
        scratch_shapes=list(scratch),
        compiler_params=GRANT,
        cost_estimate=cost,
        name=name,
    )


def blank_kernel(out):
    out[...] = jnp.zeros((8, 128), jnp.float32)


def pack_kernel(count, spans, blocks, base, out):
    last = count[0] - 1
    row = iota((8, 128), 0)
    tile = jnp.where(row == 0, spans[0, 0], base[...])
    tile = jnp.where(row == 1, blocks[0, 0].astype(jnp.float32), tile)
    tile = jnp.where(row == 2, spans[0, last], tile)
    out[...] = jnp.where(row == 3, blocks[0, last].astype(jnp.float32), tile)


def project_kernel(place, count_in, spans, blocks, taps_in, vel, table, stream, shear, out, pooled):
    count = count_in[0]
    odd = place[0] == 1

    lane = iota((128, 128), 1)
    gap = iota((128, 128), 0) - 4 * (lane % 32) - lane // 32 + 1
    pool = jnp.where((gap >= 0) & (gap < 4) & (lane < 96), 1.0, 0.0).astype(jnp.bfloat16)
    group = iota((8, 128), 1) // 32

    def tap(i, q, a):
        at = ((i * 2 + q) * 3 + a) * 3
        picked = jnp.where(group == 0, taps_in[at], jnp.where(group == 1, taps_in[at + 1], taps_in[at + 2]))
        return jnp.where(group < 3, picked * SMALL, 0.0)

    taps = {(i, q, a): tap(i, q, a) for i in range(3) for q in range(2) for a in range(3)}
    zeros = jnp.zeros((32, 256), jnp.bfloat16)
    omega = stream[...]
    spread = jnp.concatenate([omega, zeros, zeros, zeros], axis=0)
    centre = jnp.concatenate([zeros, omega, zeros, zeros] * 2, axis=0)
    first_row = iota((32, 128), 0) == 0
    last_row = iota((32, 128), 0) == 31

    planes, normals = [], []
    for c in range(CAP):
        pooled[pl.ds(PAD + c * 384, 384), :] = dot(vel[pl.ds(c * 384, 384), :], pool)
    for c in range(CAP):
        feats, centres = [], []
        for i in range(3):
            base = PAD + (c * 3 + i) * 128
            row = [pooled[pl.ds(base + j, 32, stride=4), :] for j in range(4)]
            before = jnp.where(first_row, 0.0, pooled[pl.ds(base - 1, 32, stride=4), :])
            after = jnp.where(last_row, 0.0, pooled[pl.ds(base + 4, 32, stride=4), :])
            inside = row[1] + row[2]
            head = row[0] + inside
            window = (before + head, head + row[3], inside + row[3] + after)
            for q in range(2):
                mixed = sum(
                    (window[a].reshape(4, 8, 128) * taps[i, q, a][None]).reshape(32, 128) for a in range(3)
                )
                folded = mixed + pltpu.roll(mixed, 96, 1) + pltpu.roll(mixed, 64, 1)
                feats.append(folded.astype(jnp.bfloat16))
            centres.append(jnp.concatenate(split(window[1] * SMALL), axis=1))
        planes.append(dot(jnp.concatenate(feats, axis=0), spread))
        normals.append(dot(jnp.concatenate(centres, axis=0), centre))

    def rows_of(block, channel):
        return table[block, channel * 32 : channel * 32 + 32, :].astype(jnp.float32)

    def fold(value):
        return value.reshape(4, 8, 256).sum(0)

    total = jnp.zeros((8, 256), jnp.float32)
    for c in range(CAP):
        alive = jnp.where(c < count, 1.0, 0.0)
        part = jnp.zeros((8, 256), jnp.float32)
        for i in range(3):
            for q in range(2):
                at = (i * 2 + q) * 32
                part += fold(planes[c][at : at + 32] * rows_of(blocks[0, c], 3 * i + q))
            weight = None
            if c:
                weight = spans[0, c - 1] * rows_of(blocks[0, c - 1], 3 * i + 2)
            if c + 1 < CAP:
                span = jnp.where(c + 1 < count, spans[0, c + 1], 0.0)
                down = span * rows_of(blocks[0, c + 1], 3 * i + 2)
                weight = -down if weight is None else weight - down
            part += fold(normals[c][i * 32 : i * 32 + 32] * weight)
        total += alive * part
    out[0:8, :] = total

    final = sum(jnp.where(c + 1 == count, 1.0, 0.0) * normals[c] for c in range(CAP))
    edges = (jnp.where(odd, final, normals[0]), jnp.where(odd, normals[0], final))
    found = ([], [])
    for block in range(BLOCKS):
        parts = [jnp.zeros((8, 256), jnp.float32)] * 2
        for i in range(3):
            rows = rows_of(block, 3 * i + 2)
            parts = [part + fold(edge[i * 32 : i * 32 + 32] * rows) for part, edge in zip(parts, edges)]
        for part, rows in zip(parts, found):
            rows.append(jnp.sum(part, axis=0, keepdims=True))
    out[8:16, :] = jnp.concatenate(found[0], axis=0)
    out[16:24, :] = jnp.concatenate(found[1], axis=0)

    wall = dot(shear[...], pool) * SMALL
    first = jnp.broadcast_to(jnp.sum(wall[0:4], axis=0, keepdims=True), (8, 128))
    second = jnp.broadcast_to(jnp.sum(wall[4:8], axis=0, keepdims=True), (8, 128))
    low = jnp.where(group == 0, pltpu.roll(first, 96, 1), jnp.where(group == 1, second, 0.0))
    out[24:32, :] = jnp.concatenate([low, low], axis=1)


def send_kernel(place, part, partner, out):
    odd = place[0] == 1
    tile = partner[...]
    row = iota((8, 128), 0)

    def spread(at):
        return jnp.broadcast_to(tile[at : at + 1], (8, 128))

    span = jnp.where(odd, spread(2), -spread(0))
    block = jnp.where(odd, spread(3), spread(1)).astype(jnp.int32)
    weight = jnp.where(row == block, span, 0.0)
    near = part[16:24, :] * jnp.concatenate([weight, weight], axis=1)
    coef = jnp.sum(part[0:8, :] + near, axis=0, keepdims=True)
    coef = jnp.broadcast_to(coef, (8, 256))

    def pair(value):
        high = value.astype(jnp.bfloat16).astype(jnp.float32)
        return high, value - high

    high, low = pair(coef)
    wall, wall_low = pair(part[24:32, :128])
    wall = wall + pltpu.roll(wall_low, 64, 1)
    far, far_low = pair(jnp.where(odd, -spread(0), spread(2)))
    told = jnp.where(odd, spread(1), spread(3))
    picks = (high[:, :128], high[:, 128:], low[:, :128], low[:, 128:], wall, far, far_low, told)
    small = picks[-1]
    for at in range(7):
        small = jnp.where(row == at, picks[at], small)
    outer = part[8:16, :]
    whole = jnp.concatenate([outer[:, :128], outer[:, 128:], small], axis=0).astype(jnp.bfloat16)
    for copy_at in range(out.shape[0]):
        out[copy_at] = whole


def merge_kernel(place, rows, out, wide):
    odd = place[0] == 1
    chips = rows.shape[0] // SENT
    wide[...] = rows[...].astype(jnp.float32)

    def every(at):
        return wide[pl.ds(16 + at, chips, stride=SENT), :]

    low = jnp.sum(every(0) + every(2), axis=0, keepdims=True)
    high = jnp.sum(every(1) + every(3), axis=0, keepdims=True)
    wall = every(4)
    wall = wall + pltpu.roll(wall, 64, 1)
    sub = iota((8, 128), 0)
    reach = [jnp.zeros((8, 128), jnp.float32)] * 2
    for j in range(chips):
        span = wide[SENT * j + 21 : SENT * j + 22, :] + wide[SENT * j + 22 : SENT * j + 23, :]
        block = jnp.broadcast_to(wide[SENT * j + 23 : SENT * j + 24, :], (8, 128)).astype(jnp.int32)
        weight = jnp.where(sub == block, jnp.broadcast_to(span, (8, 128)), 0.0)
        before = wide[pl.ds(SENT * (j - 1), 16), :] if j > 0 else jnp.zeros((16, 128), jnp.float32)
        after = wide[pl.ds(SENT * (j + 1), 16), :] if j + 1 < chips else jnp.zeros((16, 128), jnp.float32)
        held = jnp.where(odd, before, after)
        reach = [reach[h] + weight * held[8 * h : 8 * h + 8] for h in range(2)]
    low = low + jnp.sum(reach[0], axis=0, keepdims=True)
    high = high + jnp.sum(reach[1], axis=0, keepdims=True)
    left = iota((8, 128), 1) < 64
    wide[0:chips, :] = wall
    wall = jnp.where(left, wide[pl.ds(0, 8, stride=2), :], wide[pl.ds(1, 8, stride=2), :])
    low = jnp.broadcast_to(low, (8, 128))
    high = jnp.broadcast_to(high, (8, 128))
    low_top = low.astype(jnp.bfloat16).astype(jnp.float32)
    high_top = high.astype(jnp.bfloat16).astype(jnp.float32)
    wall_top = wall.astype(jnp.bfloat16).astype(jnp.float32)
    small = jnp.where(sub == 0, low_top, jnp.where(sub == 1, high_top, jnp.where(sub == 2, low - low_top, jnp.where(sub == 3, high - high_top, 0.0))))
    whole = jnp.concatenate([wall_top, wall - wall_top, small], axis=0).astype(jnp.bfloat16)
    for copy_at in range(out.shape[0]):
        out[copy_at] = whole


def finish_kernel(place, rows, sketch, gram, wide, full):
    wide[...] = rows[...].astype(jnp.float32)

    def across(at):
        return wide[pl.ds(at, 16, stride=2 * SENT), :]

    def both(at):
        return across(at) + across(at + 2) + across(at + SENT) + across(at + SENT + 2)

    coef = jnp.concatenate([both(16), both(17)], axis=1)
    coef_high, coef_low = split(coef)
    walls = [
        jnp.concatenate([across(at), across(at + 8)], axis=0).astype(jnp.bfloat16)
        for at in [SENT * core + r for core in range(2) for r in range(8)]
    ]
    wall = jnp.concatenate(walls, axis=1)
    product = lax.dot_general(wall, wall, (((1,), (1,)), ((), ())), preferred_element_type=jnp.float32)
    product = product[0:16] + product[16:32]
    inner = product[:, 0:16] + product[:, 16:32]
    inner_high, inner_low = split(inner)
    right = dot(inner_high, coef_high) + dot(inner_low, coef_high) + dot(inner_high, coef_low)
    right_high, right_low = split(right * (1.0 / 2048.0))
    left = jnp.concatenate([coef_high, coef_low, coef_high], axis=0)
    gram[...] = lax.dot_general(
        left,
        jnp.concatenate([right_high, right_high, right_low], axis=0),
        OVER_ROWS,
        preferred_element_type=jnp.float32,
    )
    core, chip, snap = place[0], place[1], place[2]
    at = SENT * core + chip // 2
    mine_high = across(at).astype(jnp.bfloat16)
    mine_low = across(at + 8).astype(jnp.bfloat16)
    mine = jnp.concatenate([mine_high, mine_high, mine_low], axis=0)
    full[...] = lax.dot_general(mine, left, OVER_ROWS, preferred_element_type=jnp.float32)
    base = (chip % 2) * 64 + 2 * snap
    for m in range(2):
        for x in range(2):
            sketch[m, 0, x : x + 1, :] = full[pl.ds(base + 32 * m + x, 1), :]


def per_device(velocity, plane_count, inv_span, kernels, omega_block, omega_table, omega_stream, wall_shear):
    f32, bf16 = jnp.float32, jnp.bfloat16
    chips, snaps = lax.axis_size("z"), lax.axis_size("snap")
    snap, z, core = lax.axis_index("snap"), lax.axis_index("z"), lax.axis_index("core")
    place = jnp.stack([core, z, snap]).astype(jnp.int32)
    tile = jax.ShapeDtypeStruct((8, 128), f32)
    base = call(blank_kernel, "blank", tile, [], cost=LONG)()
    own = call(pack_kernel, "pack", tile, [SMEM, SMEM, SMEM, VMEM], cost=LONG)(
        plane_count, inv_span, omega_block, base
    )
    partner = lax.ppermute(own, "core", [(0, 1), (1, 0)])
    part = call(
        project_kernel,
        "project",
        jax.ShapeDtypeStruct((32, 256), f32),
        [SMEM] * 5 + [VMEM] * 4,
        [pltpu.VMEM((ROWS + 2 * PAD, 128), f32)],
        cost=LONG,
    )(
        place,
        plane_count,
        inv_span,
        omega_block,
        kernels.reshape(-1),
        velocity.reshape(ROWS, 128),
        omega_table.reshape(BLOCKS, 288, 256),
        omega_stream,
        wall_shear.reshape(8, 128),
    )
    sent = call(send_kernel, "send", jax.ShapeDtypeStruct((chips, SENT, 128), bf16), [SMEM, VMEM, VMEM])(
        place, part, partner
    )
    got = lax.all_to_all(sent, "z", 0, 0, tiled=True).reshape(chips * SENT, 128)
    sent = call(
        merge_kernel,
        "merge",
        jax.ShapeDtypeStruct((snaps * 2, SENT, 128), bf16),
        [SMEM, VMEM],
        [pltpu.VMEM((chips * SENT, 128), f32)],
    )(place, got)
    got = lax.all_to_all(sent, ("snap", "core"), 0, 0, tiled=True).reshape(snaps * 2 * SENT, 128)
    return call(
        finish_kernel,
        "finish",
        (jax.ShapeDtypeStruct((2, 1, 2, 256), f32), jax.ShapeDtypeStruct((256, 256), f32)),
        [SMEM, VMEM],
        [pltpu.VMEM((snaps * 2 * SENT, 128), f32), pltpu.VMEM((128, 256), f32)],
    )(place, got)


def solution(mesh):
    chips = mesh.shape["plane"] // 2
    fine = Mesh(mesh.devices.reshape(mesh.shape["snap"], chips, 2), ("snap", "z", "core"))
    plane = ("z", "core")
    return jax.shard_map(
        per_device,
        mesh=fine,
        in_specs=(
            P("snap", plane, None, None, None),
            P(plane),
            P(plane, None),
            P(),
            P(plane, None),
            P(),
            P(),
            P("snap", None, plane, None),
        ),
        out_specs=(P(None, plane, "snap", None), P()),
        check_vma=False,
    )
```

```python
import jax
import jax.numpy as jnp
from jax import lax
from jax.experimental import pallas as pl
from jax.experimental.pallas import tpu as pltpu
from jax.sharding import Mesh, PartitionSpec as P

CAP = 4
BLOCKS = 8
ROWS = 1536
PAD = 8
SENT = 24
SMALL = 1.0 / 16.0
LONG = pl.CostEstimate(flops=10**10, bytes_accessed=10**7, transcendentals=0)
GRANT = pltpu.CompilerParams(vmem_limit_bytes=8 << 20)
VMEM = pl.BlockSpec(memory_space=pltpu.VMEM)
OVER_ROWS = (((0,), (0,)), ((), ()))


def iota(shape, dim):
    return lax.broadcasted_iota(jnp.int32, shape, dim)


def split(value):
    high = value.astype(jnp.bfloat16)
    low = (value - high.astype(jnp.float32)).astype(jnp.bfloat16)
    return high, low


def dot(left, right):
    return jnp.dot(left, right, preferred_element_type=jnp.float32)


def call(kernel, name, out, ins, scratch=(), cost=None):
    return pl.pallas_call(
        kernel,
        out_shape=out,
        in_specs=ins,
        out_specs=jax.tree.map(lambda _: VMEM, out),
        scratch_shapes=list(scratch),
        compiler_params=GRANT,
        cost_estimate=cost,
        name=name,
    )


def blank_kernel(out):
    out[...] = jnp.zeros((8, 128), jnp.float32)


def pack_kernel(count, spans, blocks, base, out):
    row = iota((8, 128), 0)
    last = iota((1, CAP), 1) == count[:, 0:CAP] - 1
    marks = blocks[...].astype(jnp.float32)
    tile = base[...]
    for at, values in ((0, spans[...]), (1, marks)):
        final = jnp.sum(jnp.where(last, values, 0.0), axis=1, keepdims=True)
        tile = jnp.where(row == at, jnp.broadcast_to(values[:, 0:1], (8, 128)), tile)
        tile = jnp.where(row == at + 2, jnp.broadcast_to(final, (8, 128)), tile)
    out[...] = tile


def project_kernel(
    place, count_vec, spans_vec, blocks_vec, taps_vec, vel, table, stream, shear, out, pooled, count_in, spans, blocks, taps_in, sems
):
    pairs = ((taps_vec, taps_in), (count_vec, count_in), (spans_vec, spans), (blocks_vec, blocks))
    copies = [pltpu.make_async_copy(source, target, sems.at[at]) for at, (source, target) in enumerate(pairs)]
    for copy in copies:
        copy.start()
    odd = jnp.broadcast_to(place[0:1, 0:1], (96, 256)) == 1

    lane = iota((128, 128), 1)
    gap = iota((128, 128), 0) - 4 * (lane % 32) - lane // 32 + 1
    pool = jnp.where((gap >= 0) & (gap < 4) & (lane < 96), 1.0, 0.0).astype(jnp.bfloat16)
    group = iota((8, 128), 1) // 32

    zeros = jnp.zeros((32, 256), jnp.bfloat16)
    omega = stream[...]
    spread = jnp.concatenate([omega, zeros, zeros, zeros], axis=0)
    centre = jnp.concatenate([zeros, omega, zeros, zeros] * 2, axis=0)
    first_row = iota((32, 128), 0) == 0
    last_row = iota((32, 128), 0) == 31

    planes, normals = [], []
    for c in range(CAP):
        pooled[pl.ds(PAD + c * 384, 384), :] = dot(vel[pl.ds(c * 384, 384), :], pool)
    for copy in copies:
        copy.wait()
    count = count_in[0, 0]

    def tap(i, q, a):
        at = ((i * 2 + q) * 3 + a) * 3
        picked = jnp.where(group == 0, taps_in[at], jnp.where(group == 1, taps_in[at + 1], taps_in[at + 2]))
        return jnp.where(group < 3, picked * SMALL, 0.0)

    taps = {(i, q, a): tap(i, q, a) for i in range(3) for q in range(2) for a in range(3)}
    for c in range(CAP):
        feats, centres = [], []
        for i in range(3):
            base = PAD + (c * 3 + i) * 128
            row = [pooled[pl.ds(base + j, 32, stride=4), :] for j in range(4)]
            before = jnp.where(first_row, 0.0, pooled[pl.ds(base - 1, 32, stride=4), :])
            after = jnp.where(last_row, 0.0, pooled[pl.ds(base + 4, 32, stride=4), :])
            inside = row[1] + row[2]
            head = row[0] + inside
            window = (before + head, head + row[3], inside + row[3] + after)
            for q in range(2):
                mixed = sum(
                    (window[a].reshape(4, 8, 128) * taps[i, q, a][None]).reshape(32, 128) for a in range(3)
                )
                folded = mixed + pltpu.roll(mixed, 96, 1) + pltpu.roll(mixed, 64, 1)
                feats.append(folded.astype(jnp.bfloat16))
            centres.append(jnp.concatenate(split(window[1] * SMALL), axis=1))
        planes.append(dot(jnp.concatenate(feats, axis=0), spread))
        normals.append(dot(jnp.concatenate(centres, axis=0), centre))

    def rows_of(block, channel):
        return table[block, channel * 32 : channel * 32 + 32, :].astype(jnp.float32)

    def fold(value):
        return value.reshape(4, 8, 256).sum(0)

    total = jnp.zeros((8, 256), jnp.float32)
    for c in range(CAP):
        alive = jnp.where(c < count, 1.0, 0.0)
        part = jnp.zeros((8, 256), jnp.float32)
        for i in range(3):
            for q in range(2):
                at = (i * 2 + q) * 32
                part += fold(planes[c][at : at + 32] * rows_of(blocks[0, c], 3 * i + q))
            weight = None
            if c:
                weight = spans[0, c - 1] * rows_of(blocks[0, c - 1], 3 * i + 2)
            if c + 1 < CAP:
                span = jnp.where(c + 1 < count, spans[0, c + 1], 0.0)
                down = span * rows_of(blocks[0, c + 1], 3 * i + 2)
                weight = -down if weight is None else weight - down
            part += fold(normals[c][i * 32 : i * 32 + 32] * weight)
        total += alive * part
    out[0:8, :] = total

    final = sum(jnp.where(c + 1 == count, 1.0, 0.0) * normals[c] for c in range(CAP))
    edges = (jnp.where(odd, final, normals[0]), jnp.where(odd, normals[0], final))
    found = ([], [])
    for block in range(BLOCKS):
        parts = [jnp.zeros((8, 256), jnp.float32)] * 2
        for i in range(3):
            rows = rows_of(block, 3 * i + 2)
            parts = [part + fold(edge[i * 32 : i * 32 + 32] * rows) for part, edge in zip(parts, edges)]
        for part, rows in zip(parts, found):
            rows.append(jnp.sum(part, axis=0, keepdims=True))
    out[8:16, :] = jnp.concatenate(found[0], axis=0)
    out[16:24, :] = jnp.concatenate(found[1], axis=0)

    wall = dot(shear[...], pool) * SMALL
    first = jnp.broadcast_to(jnp.sum(wall[0:4], axis=0, keepdims=True), (8, 128))
    second = jnp.broadcast_to(jnp.sum(wall[4:8], axis=0, keepdims=True), (8, 128))
    low = jnp.where(group == 0, pltpu.roll(first, 96, 1), jnp.where(group == 1, second, 0.0))
    out[24:32, :] = jnp.concatenate([low, low], axis=1)


def send_kernel(place, part, partner, out):
    odd = jnp.broadcast_to(place[0:1, :], (8, 128)) == 1
    tile = partner[...]
    row = iota((8, 128), 0)

    def spread(at):
        return jnp.broadcast_to(tile[at : at + 1], (8, 128))

    span = jnp.where(odd, spread(2), -spread(0))
    block = jnp.where(odd, spread(3), spread(1)).astype(jnp.int32)
    weight = jnp.where(row == block, span, 0.0)
    near = part[16:24, :] * jnp.concatenate([weight, weight], axis=1)
    coef = jnp.sum(part[0:8, :] + near, axis=0, keepdims=True)
    coef = jnp.broadcast_to(coef, (8, 256))

    def pair(value):
        high = value.astype(jnp.bfloat16).astype(jnp.float32)
        return high, value - high

    high, low = pair(coef)
    wall, wall_low = pair(part[24:32, :128])
    wall = wall + pltpu.roll(wall_low, 64, 1)
    far, far_low = pair(jnp.where(odd, -spread(0), spread(2)))
    told = jnp.where(odd, spread(1), spread(3))
    picks = (high[:, :128], high[:, 128:], low[:, :128], low[:, 128:], wall, far, far_low, told)
    small = picks[-1]
    for at in range(7):
        small = jnp.where(row == at, picks[at], small)
    outer = part[8:16, :]
    whole = jnp.concatenate([outer[:, :128], outer[:, 128:], small], axis=0).astype(jnp.bfloat16)
    for copy_at in range(out.shape[0]):
        out[copy_at] = whole


def merge_kernel(place, rows, out, wide):
    odd = jnp.broadcast_to(place[0:1, :], (16, 128)) == 1
    chips = rows.shape[0] // SENT
    wide[...] = rows[...].astype(jnp.float32)

    def every(at):
        return wide[pl.ds(16 + at, chips, stride=SENT), :]

    low = jnp.sum(every(0) + every(2), axis=0, keepdims=True)
    high = jnp.sum(every(1) + every(3), axis=0, keepdims=True)
    wall = every(4)
    wall = wall + pltpu.roll(wall, 64, 1)
    sub = iota((8, 128), 0)
    reach = [jnp.zeros((8, 128), jnp.float32)] * 2
    for j in range(chips):
        span = wide[SENT * j + 21 : SENT * j + 22, :] + wide[SENT * j + 22 : SENT * j + 23, :]
        block = jnp.broadcast_to(wide[SENT * j + 23 : SENT * j + 24, :], (8, 128)).astype(jnp.int32)
        weight = jnp.where(sub == block, jnp.broadcast_to(span, (8, 128)), 0.0)
        before = wide[pl.ds(SENT * (j - 1), 16), :] if j > 0 else jnp.zeros((16, 128), jnp.float32)
        after = wide[pl.ds(SENT * (j + 1), 16), :] if j + 1 < chips else jnp.zeros((16, 128), jnp.float32)
        held = jnp.where(odd, before, after)
        reach = [reach[h] + weight * held[8 * h : 8 * h + 8] for h in range(2)]
    low = low + jnp.sum(reach[0], axis=0, keepdims=True)
    high = high + jnp.sum(reach[1], axis=0, keepdims=True)
    left = iota((8, 128), 1) < 64
    wide[0:chips, :] = wall
    wall = jnp.where(left, wide[pl.ds(0, 8, stride=2), :], wide[pl.ds(1, 8, stride=2), :])
    low = jnp.broadcast_to(low, (8, 128))
    high = jnp.broadcast_to(high, (8, 128))
    low_top = low.astype(jnp.bfloat16).astype(jnp.float32)
    high_top = high.astype(jnp.bfloat16).astype(jnp.float32)
    wall_top = wall.astype(jnp.bfloat16).astype(jnp.float32)
    small = jnp.where(sub == 0, low_top, jnp.where(sub == 1, high_top, jnp.where(sub == 2, low - low_top, jnp.where(sub == 3, high - high_top, 0.0))))
    whole = jnp.concatenate([wall_top, wall - wall_top, small], axis=0).astype(jnp.bfloat16)
    for copy_at in range(out.shape[0]):
        out[copy_at] = whole


def finish_kernel(place, rows, sketch, gram, wide):
    wide[...] = rows[...].astype(jnp.float32)

    def across(at):
        return wide[pl.ds(at, 16, stride=2 * SENT), :]

    def both(at):
        return across(at) + across(at + 2) + across(at + SENT) + across(at + SENT + 2)

    coef = jnp.concatenate([both(16), both(17)], axis=1)
    coef_high, coef_low = split(coef)
    walls = [
        jnp.concatenate([across(at), across(at + 8)], axis=0).astype(jnp.bfloat16)
        for at in [SENT * core + r for core in range(2) for r in range(8)]
    ]
    wall = jnp.concatenate(walls, axis=1)
    product = lax.dot_general(wall, wall, (((1,), (1,)), ((), ())), preferred_element_type=jnp.float32)
    product = product[0:16] + product[16:32]
    inner = product[:, 0:16] + product[:, 16:32]
    inner_high, inner_low = split(inner)
    right = dot(inner_high, coef_high) + dot(inner_low, coef_high) + dot(inner_high, coef_low)
    right_high, right_low = split(right * (1.0 / 2048.0))
    left = jnp.concatenate([coef_high, coef_low, coef_high], axis=0)
    gram[...] = lax.dot_general(
        left,
        jnp.concatenate([right_high, right_high, right_low], axis=0),
        OVER_ROWS,
        preferred_element_type=jnp.float32,
    )
    core, chip, snap = (jnp.broadcast_to(place[at : at + 1, :], (16, 128)) for at in range(3))
    row_at = core * 8 + lax.shift_right_logical(chip, 1)
    mine = jnp.zeros((16, 128), jnp.float32)
    for c in range(2):
        for r in range(8):
            at = SENT * c + r
            mine = jnp.where(row_at == c * 8 + r, across(at) + across(at + 8), mine)
    target = iota((16, 128), 1) - (chip & 1) * 64 - 2 * snap
    for m in range(2):
        for x in range(2):
            column = jnp.sum(jnp.where(target == 32 * m + x, mine, 0.0), axis=1, keepdims=True)
            sketch[m, 0, x : x + 1, :] = jnp.sum(column * coef, axis=0, keepdims=True)


def per_device(velocity, plane_count, inv_span, kernels, omega_block, omega_table, omega_stream, wall_shear):
    f32, bf16 = jnp.float32, jnp.bfloat16
    chips, snaps = lax.axis_size("z"), lax.axis_size("snap")
    snap, z, core = lax.axis_index("snap"), lax.axis_index("z"), lax.axis_index("core")
    row = iota((8, 128), 0)
    place = jnp.where(row == 0, core, jnp.where(row == 1, z, snap)).astype(jnp.int32)
    count = jnp.broadcast_to(plane_count.reshape(1, 1), (1, 128))
    tile = jax.ShapeDtypeStruct((8, 128), f32)
    base = call(blank_kernel, "blank", tile, [], cost=LONG)()
    own = call(pack_kernel, "pack", tile, [VMEM] * 4, cost=LONG)(
        count, inv_span, omega_block, base
    )
    partner = lax.ppermute(own, "core", [(0, 1), (1, 0)])
    part = call(
        project_kernel,
        "project",
        jax.ShapeDtypeStruct((32, 256), f32),
        [VMEM] * 9,
        [
            pltpu.VMEM((ROWS + 2 * PAD, 128), f32),
            pltpu.SMEM((1, 128), jnp.int32),
            pltpu.SMEM((1, CAP), f32),
            pltpu.SMEM((1, CAP), jnp.int32),
            pltpu.SMEM((54,), f32),
            pltpu.SemaphoreType.DMA((4,)),
        ],
        cost=LONG,
    )(
        place,
        count,
        inv_span,
        omega_block,
        kernels.reshape(-1),
        velocity.reshape(ROWS, 128),
        omega_table.reshape(BLOCKS, 288, 256),
        omega_stream,
        wall_shear.reshape(8, 128),
    )
    sent = call(send_kernel, "send", jax.ShapeDtypeStruct((chips, SENT, 128), bf16), [VMEM] * 3)(
        place, part, partner
    )
    got = lax.all_to_all(sent, "z", 0, 0, tiled=True).reshape(chips * SENT, 128)
    sent = call(
        merge_kernel,
        "merge",
        jax.ShapeDtypeStruct((snaps * 2, SENT, 128), bf16),
        [VMEM, VMEM],
        [pltpu.VMEM((chips * SENT, 128), f32)],
    )(place, got)
    got = lax.all_to_all(sent, ("snap", "core"), 0, 0, tiled=True).reshape(snaps * 2 * SENT, 128)
    return call(
        finish_kernel,
        "finish",
        (jax.ShapeDtypeStruct((2, 1, 2, 256), f32), jax.ShapeDtypeStruct((256, 256), f32)),
        [VMEM, VMEM],
        [pltpu.VMEM((snaps * 2 * SENT, 128), f32)],
    )(place, got)


def solution(mesh):
    chips = mesh.shape["plane"] // 2
    fine = Mesh(mesh.devices.reshape(mesh.shape["snap"], chips, 2), ("snap", "z", "core"))
    plane = ("z", "core")
    return jax.shard_map(
        per_device,
        mesh=fine,
        in_specs=(
            P("snap", plane, None, None, None),
            P(plane),
            P(plane, None),
            P(),
            P(plane, None),
            P(),
            P(),
            P("snap", None, plane, None),
        ),
        out_specs=(P(None, plane, "snap", None), P()),
        check_vma=False,
    )
```

```python
import jax
import jax.numpy as jnp
from jax import lax
from jax.experimental import pallas as pl
from jax.experimental.pallas import tpu as pltpu
from jax.sharding import Mesh, PartitionSpec as P

CAP = 4
BLOCKS = 8
ROWS = 1536
PAD = 8
SENT = 24
SMALL = 1.0 / 16.0
LONG = pl.CostEstimate(flops=10**10, bytes_accessed=10**7, transcendentals=0)
GRANT = pltpu.CompilerParams(vmem_limit_bytes=8 << 20)
SPREAD = pltpu.CompilerParams(vmem_limit_bytes=8 << 20)
VMEM = pl.BlockSpec(memory_space=pltpu.VMEM)
OVER_ROWS = (((0,), (0,)), ((), ()))


def iota(shape, dim):
    return lax.broadcasted_iota(jnp.int32, shape, dim)


def split(value):
    high = value.astype(jnp.bfloat16)
    low = (value - high.astype(jnp.float32)).astype(jnp.bfloat16)
    return high, low


def dot(left, right):
    return jnp.dot(left, right, preferred_element_type=jnp.float32)


def call(kernel, name, out, ins, scratch=(), cost=None, params=GRANT):
    return pl.pallas_call(
        kernel,
        out_shape=out,
        in_specs=ins,
        out_specs=jax.tree.map(lambda _: VMEM, out),
        scratch_shapes=list(scratch),
        compiler_params=params,
        cost_estimate=cost,
        name=name,
    )


def blank_kernel(out):
    out[...] = jnp.zeros((8, 128), jnp.float32)


def pack_kernel(count, spans, blocks, base, out):
    row = iota((8, 128), 0)
    last = iota((1, CAP), 1) == count[:, 0:CAP] - 1
    marks = blocks[...].astype(jnp.float32)
    tile = base[...]
    for at, values in ((0, spans[...]), (1, marks)):
        final = jnp.sum(jnp.where(last, values, 0.0), axis=1, keepdims=True)
        tile = jnp.where(row == at, jnp.broadcast_to(values[:, 0:1], (8, 128)), tile)
        tile = jnp.where(row == at + 2, jnp.broadcast_to(final, (8, 128)), tile)
    out[...] = tile


def project_kernel(
    place, count_vec, spans_vec, blocks_vec, taps_vec, vel, table, stream, shear, out, pooled, count_in, spans, blocks, taps_in, sems
):
    pairs = ((taps_vec, taps_in), (count_vec, count_in), (spans_vec, spans), (blocks_vec, blocks))
    copies = [pltpu.make_async_copy(source, target, sems.at[at]) for at, (source, target) in enumerate(pairs)]
    for copy in copies:
        copy.start()
    odd = jnp.broadcast_to(place[0:1, 0:1], (96, 256)) == 1

    lane = iota((128, 128), 1)
    gap = iota((128, 128), 0) - 4 * (lane % 32) - lane // 32 + 1
    pool = jnp.where((gap >= 0) & (gap < 4) & (lane < 96), 1.0, 0.0).astype(jnp.bfloat16)
    group = iota((8, 128), 1) // 32

    zeros = jnp.zeros((32, 256), jnp.bfloat16)
    omega = stream[...]
    spread = jnp.concatenate([omega, zeros, zeros, zeros], axis=0)
    centre = jnp.concatenate([zeros, omega, zeros, zeros] * 2, axis=0)
    first_row = iota((32, 128), 0) == 0
    last_row = iota((32, 128), 0) == 31

    for c in range(CAP):
        pooled[pl.ds(PAD + c * 384, 384), :] = dot(vel[pl.ds(c * 384, 384), :], pool)

    def rows_at(c, i):
        base = PAD + (c * 3 + i) * 128
        return base, [pooled[pl.ds(base + j, 32, stride=4), :] for j in range(4)]

    normals = []
    for c in range(CAP):
        centres = []
        for i in range(3):
            row = rows_at(c, i)[1]
            centres.append(jnp.concatenate(split((row[0] + row[1] + row[2] + row[3]) * SMALL), axis=1))
        normals.append(dot(jnp.concatenate(centres, axis=0), centre))

    def rows_of(block, channel):
        return table[block, channel * 32 : channel * 32 + 32, :].astype(jnp.float32)

    def fold(value):
        return value.reshape(4, 8, 256).sum(0)

    counts = jnp.concatenate([count_vec[...], count_vec[...]], axis=1)
    final = sum(jnp.where(counts == c + 1, 1.0, 0.0) * normals[c] for c in range(CAP))
    edges = (jnp.where(odd, final, normals[0]), jnp.where(odd, normals[0], final))
    found = ([], [])
    for block in range(BLOCKS):
        parts = [jnp.zeros((8, 256), jnp.float32)] * 2
        for i in range(3):
            rows = rows_of(block, 3 * i + 2)
            parts = [part + fold(edge[i * 32 : i * 32 + 32] * rows) for part, edge in zip(parts, edges)]
        for part, rows in zip(parts, found):
            rows.append(jnp.sum(part, axis=0, keepdims=True))
    out[8:16, :] = jnp.concatenate(found[0], axis=0)
    out[16:24, :] = jnp.concatenate(found[1], axis=0)

    wall = dot(shear[...], pool) * SMALL
    first = jnp.broadcast_to(jnp.sum(wall[0:4], axis=0, keepdims=True), (8, 128))
    second = jnp.broadcast_to(jnp.sum(wall[4:8], axis=0, keepdims=True), (8, 128))
    low = jnp.where(group == 0, pltpu.roll(first, 96, 1), jnp.where(group == 1, second, 0.0))
    out[24:32, :] = jnp.concatenate([low, low], axis=1)

    for copy in copies:
        copy.wait()
    count = count_in[0, 0]

    def tap(i, q, a):
        at = ((i * 2 + q) * 3 + a) * 3
        picked = jnp.where(group == 0, taps_in[at], jnp.where(group == 1, taps_in[at + 1], taps_in[at + 2]))
        return jnp.where(group < 3, picked * SMALL, 0.0)

    taps = {(i, q, a): tap(i, q, a) for i in range(3) for q in range(2) for a in range(3)}

    planes = []
    for c in range(CAP):
        feats = []
        for i in range(3):
            base, row = rows_at(c, i)
            before = jnp.where(first_row, 0.0, pooled[pl.ds(base - 1, 32, stride=4), :])
            after = jnp.where(last_row, 0.0, pooled[pl.ds(base + 4, 32, stride=4), :])
            inside = row[1] + row[2]
            head = row[0] + inside
            window = (before + head, head + row[3], inside + row[3] + after)
            for q in range(2):
                mixed = sum(
                    (window[a].reshape(4, 8, 128) * taps[i, q, a][None]).reshape(32, 128) for a in range(3)
                )
                folded = mixed + pltpu.roll(mixed, 96, 1) + pltpu.roll(mixed, 64, 1)
                feats.append(folded.astype(jnp.bfloat16))
        planes.append(dot(jnp.concatenate(feats, axis=0), spread))

    total = jnp.zeros((8, 256), jnp.float32)
    for c in range(CAP):
        alive = jnp.where(c < count, 1.0, 0.0)
        part = jnp.zeros((8, 256), jnp.float32)
        for i in range(3):
            for q in range(2):
                at = (i * 2 + q) * 32
                part += fold(planes[c][at : at + 32] * rows_of(blocks[0, c], 3 * i + q))
            weight = None
            if c:
                weight = spans[0, c - 1] * rows_of(blocks[0, c - 1], 3 * i + 2)
            if c + 1 < CAP:
                span = jnp.where(c + 1 < count, spans[0, c + 1], 0.0)
                down = span * rows_of(blocks[0, c + 1], 3 * i + 2)
                weight = -down if weight is None else weight - down
            part += fold(normals[c][i * 32 : i * 32 + 32] * weight)
        total += alive * part
    out[0:8, :] = total


def send_kernel(place, part, partner, out):
    odd = jnp.broadcast_to(place[0:1, :], (8, 128)) == 1
    tile = partner[...]
    row = iota((8, 128), 0)

    def spread(at):
        return jnp.broadcast_to(tile[at : at + 1], (8, 128))

    span = jnp.where(odd, spread(2), -spread(0))
    block = jnp.where(odd, spread(3), spread(1)).astype(jnp.int32)
    weight = jnp.where(row == block, span, 0.0)
    near = part[16:24, :] * jnp.concatenate([weight, weight], axis=1)
    coef = jnp.sum(part[0:8, :] + near, axis=0, keepdims=True)
    coef = jnp.broadcast_to(coef, (8, 256))

    def pair(value):
        high = value.astype(jnp.bfloat16).astype(jnp.float32)
        return high, value - high

    high, low = pair(coef)
    wall, wall_low = pair(part[24:32, :128])
    wall = wall + pltpu.roll(wall_low, 64, 1)
    far, far_low = pair(jnp.where(odd, -spread(0), spread(2)))
    told = jnp.where(odd, spread(1), spread(3))
    picks = (high[:, :128], high[:, 128:], low[:, :128], low[:, 128:], wall, far, far_low, told)
    small = picks[-1]
    for at in range(7):
        small = jnp.where(row == at, picks[at], small)
    outer = part[8:16, :]
    whole = jnp.concatenate([outer[:, :128], outer[:, 128:], small], axis=0).astype(jnp.bfloat16)
    for copy_at in range(out.shape[0]):
        out[copy_at] = whole


def merge_kernel(place, rows, out, wide):
    odd = jnp.broadcast_to(place[0:1, :], (16, 128)) == 1
    chips = rows.shape[0] // SENT
    wide[...] = rows[...].astype(jnp.float32)

    def every(at):
        return wide[pl.ds(16 + at, chips, stride=SENT), :]

    low = jnp.sum(every(0) + every(2), axis=0, keepdims=True)
    high = jnp.sum(every(1) + every(3), axis=0, keepdims=True)
    wall = every(4)
    wall = wall + pltpu.roll(wall, 64, 1)
    sub = iota((8, 128), 0)
    reach = [jnp.zeros((8, 128), jnp.float32)] * 2
    for j in range(chips):
        span = wide[SENT * j + 21 : SENT * j + 22, :] + wide[SENT * j + 22 : SENT * j + 23, :]
        block = jnp.broadcast_to(wide[SENT * j + 23 : SENT * j + 24, :], (8, 128)).astype(jnp.int32)
        weight = jnp.where(sub == block, jnp.broadcast_to(span, (8, 128)), 0.0)
        before = wide[pl.ds(SENT * (j - 1), 16), :] if j > 0 else jnp.zeros((16, 128), jnp.float32)
        after = wide[pl.ds(SENT * (j + 1), 16), :] if j + 1 < chips else jnp.zeros((16, 128), jnp.float32)
        held = jnp.where(odd, before, after)
        reach = [reach[h] + weight * held[8 * h : 8 * h + 8] for h in range(2)]
    low = low + jnp.sum(reach[0], axis=0, keepdims=True)
    high = high + jnp.sum(reach[1], axis=0, keepdims=True)
    left = iota((8, 128), 1) < 64
    wide[0:chips, :] = wall
    wall = jnp.where(left, wide[pl.ds(0, 8, stride=2), :], wide[pl.ds(1, 8, stride=2), :])
    low = jnp.broadcast_to(low, (8, 128))
    high = jnp.broadcast_to(high, (8, 128))
    low_top = low.astype(jnp.bfloat16).astype(jnp.float32)
    high_top = high.astype(jnp.bfloat16).astype(jnp.float32)
    wall_top = wall.astype(jnp.bfloat16).astype(jnp.float32)
    small = jnp.where(sub == 0, low_top, jnp.where(sub == 1, high_top, jnp.where(sub == 2, low - low_top, jnp.where(sub == 3, high - high_top, 0.0))))
    whole = jnp.concatenate([wall_top, wall - wall_top, small], axis=0).astype(jnp.bfloat16)
    for copy_at in range(out.shape[0]):
        out[copy_at] = whole


def finish_kernel(place, rows, sketch, gram, wide):
    wide[...] = rows[...].astype(jnp.float32)

    def across(at):
        return wide[pl.ds(at, 16, stride=2 * SENT), :]

    def both(at):
        return across(at) + across(at + 2) + across(at + SENT) + across(at + SENT + 2)

    coef = jnp.concatenate([both(16), both(17)], axis=1)
    coef_high, coef_low = split(coef)
    walls = [
        jnp.concatenate([across(at), across(at + 8)], axis=0).astype(jnp.bfloat16)
        for at in [SENT * core + r for core in range(2) for r in range(8)]
    ]
    wall = jnp.concatenate(walls, axis=1)
    product = lax.dot_general(wall, wall, (((1,), (1,)), ((), ())), preferred_element_type=jnp.float32)
    product = product[0:16] + product[16:32]
    inner = product[:, 0:16] + product[:, 16:32]
    inner_high, inner_low = split(inner)
    right = dot(inner_high, coef_high) + dot(inner_low, coef_high) + dot(inner_high, coef_low)
    right_high, right_low = split(right * (1.0 / 2048.0))
    left = jnp.concatenate([coef_high, coef_low, coef_high], axis=0)
    gram[...] = lax.dot_general(
        left,
        jnp.concatenate([right_high, right_high, right_low], axis=0),
        OVER_ROWS,
        preferred_element_type=jnp.float32,
    )
    core, chip, snap = (jnp.broadcast_to(place[at : at + 1, :], (16, 128)) for at in range(3))
    row_at = core * 8 + lax.shift_right_logical(chip, 1)
    mine = jnp.zeros((16, 128), jnp.float32)
    for c in range(2):
        for r in range(8):
            at = SENT * c + r
            mine = jnp.where(row_at == c * 8 + r, across(at) + across(at + 8), mine)
    target = iota((16, 128), 1) - (chip & 1) * 64 - 2 * snap
    for m in range(2):
        for x in range(2):
            column = jnp.sum(jnp.where(target == 32 * m + x, mine, 0.0), axis=1, keepdims=True)
            sketch[m, 0, x : x + 1, :] = jnp.sum(column * coef, axis=0, keepdims=True)


def per_device(velocity, plane_count, inv_span, kernels, omega_block, omega_table, omega_stream, wall_shear):
    f32, bf16 = jnp.float32, jnp.bfloat16
    chips, snaps = lax.axis_size("z"), lax.axis_size("snap")
    snap, z, core = lax.axis_index("snap"), lax.axis_index("z"), lax.axis_index("core")
    row = iota((8, 128), 0)
    place = jnp.where(row == 0, core, jnp.where(row == 1, z, snap)).astype(jnp.int32)
    count = jnp.broadcast_to(plane_count.reshape(1, 1), (1, 128))
    tile = jax.ShapeDtypeStruct((8, 128), f32)
    base = call(blank_kernel, "blank", tile, [], cost=LONG)()
    own = call(pack_kernel, "pack", tile, [VMEM] * 4, cost=LONG)(
        count, inv_span, omega_block, base
    )
    partner = lax.ppermute(own, "core", [(0, 1), (1, 0)])
    part = call(
        project_kernel,
        "project",
        jax.ShapeDtypeStruct((32, 256), f32),
        [VMEM] * 9,
        [
            pltpu.VMEM((ROWS + 2 * PAD, 128), f32),
            pltpu.SMEM((1, 128), jnp.int32),
            pltpu.SMEM((1, CAP), f32),
            pltpu.SMEM((1, CAP), jnp.int32),
            pltpu.SMEM((54,), f32),
            pltpu.SemaphoreType.DMA((4,)),
        ],
        cost=LONG,
        params=SPREAD,
    )(
        place,
        count,
        inv_span,
        omega_block,
        kernels.reshape(-1),
        velocity.reshape(ROWS, 128),
        omega_table.reshape(BLOCKS, 288, 256),
        omega_stream,
        wall_shear.reshape(8, 128),
    )
    sent = call(send_kernel, "send", jax.ShapeDtypeStruct((chips, SENT, 128), bf16), [VMEM] * 3)(
        place, part, partner
    )
    got = lax.all_to_all(sent, "z", 0, 0, tiled=True).reshape(chips * SENT, 128)
    sent = call(
        merge_kernel,
        "merge",
        jax.ShapeDtypeStruct((snaps * 2, SENT, 128), bf16),
        [VMEM, VMEM],
        [pltpu.VMEM((chips * SENT, 128), f32)],
    )(place, got)
    got = lax.all_to_all(sent, ("snap", "core"), 0, 0, tiled=True).reshape(snaps * 2 * SENT, 128)
    return call(
        finish_kernel,
        "finish",
        (jax.ShapeDtypeStruct((2, 1, 2, 256), f32), jax.ShapeDtypeStruct((256, 256), f32)),
        [VMEM, VMEM],
        [pltpu.VMEM((snaps * 2 * SENT, 128), f32)],
    )(place, got)


def solution(mesh):
    chips = mesh.shape["plane"] // 2
    fine = Mesh(mesh.devices.reshape(mesh.shape["snap"], chips, 2), ("snap", "z", "core"))
    plane = ("z", "core")
    return jax.shard_map(
        per_device,
        mesh=fine,
        in_specs=(
            P("snap", plane, None, None, None),
            P(plane),
            P(plane, None),
            P(),
            P(plane, None),
            P(),
            P(),
            P("snap", None, plane, None),
        ),
        out_specs=(P(None, plane, "snap", None), P()),
        check_vma=False,
    )
```

```python
import jax
import jax.numpy as jnp
from jax import lax
from jax.experimental import pallas as pl
from jax.experimental.pallas import tpu as pltpu
from jax.sharding import Mesh, PartitionSpec as P

CAP = 4
BLOCKS = 8
ROWS = 1536
PAD = 8
SENT = 24
SMALL = 1.0 / 16.0
LONG = pl.CostEstimate(flops=10**10, bytes_accessed=10**7, transcendentals=0)
GRANT = pltpu.CompilerParams(vmem_limit_bytes=8 << 20)
SPREAD = pltpu.CompilerParams(vmem_limit_bytes=8 << 20)
VMEM = pl.BlockSpec(memory_space=pltpu.VMEM)
OVER_ROWS = (((0,), (0,)), ((), ()))


def iota(shape, dim):
    return lax.broadcasted_iota(jnp.int32, shape, dim)


def split(value):
    high = value.astype(jnp.bfloat16)
    low = (value - high.astype(jnp.float32)).astype(jnp.bfloat16)
    return high, low


def dot(left, right):
    return jnp.dot(left, right, preferred_element_type=jnp.float32)


def call(kernel, name, out, ins, scratch=(), cost=None, params=GRANT):
    return pl.pallas_call(
        kernel,
        out_shape=out,
        in_specs=ins,
        out_specs=jax.tree.map(lambda _: VMEM, out),
        scratch_shapes=list(scratch),
        compiler_params=params,
        cost_estimate=cost,
        name=name,
    )


def blank_kernel(out):
    out[...] = jnp.zeros((8, 128), jnp.float32)


def pack_kernel(count, spans, blocks, base, out):
    row = iota((8, 128), 0)
    last = iota((1, CAP), 1) == count[:, 0:CAP] - 1
    marks = blocks[...].astype(jnp.float32)
    tile = base[...]
    for at, values in ((0, spans[...]), (1, marks)):
        final = jnp.sum(jnp.where(last, values, 0.0), axis=1, keepdims=True)
        tile = jnp.where(row == at, jnp.broadcast_to(values[:, 0:1], (8, 128)), tile)
        tile = jnp.where(row == at + 2, jnp.broadcast_to(final, (8, 128)), tile)
    out[...] = tile


def project_kernel(
    count_vec, spans_vec, blocks_vec, taps_in, vel, table, stream, shear, out, pooled, count_in, spans, blocks, sems
):
    pairs = ((count_vec, count_in), (spans_vec, spans), (blocks_vec, blocks))
    copies = [pltpu.make_async_copy(source, target, sems.at[at]) for at, (source, target) in enumerate(pairs)]
    for copy in copies:
        copy.start()
    odd = lax.axis_index("core") == 1

    lane = iota((128, 128), 1)
    gap = iota((128, 128), 0) - 4 * (lane % 32) - lane // 32 + 1
    pool = jnp.where((gap >= 0) & (gap < 4) & (lane < 96), 1.0, 0.0).astype(jnp.bfloat16)
    group = iota((8, 128), 1) // 32

    zeros = jnp.zeros((32, 256), jnp.bfloat16)
    omega = stream[...]
    spread = jnp.concatenate([omega, zeros, zeros, zeros], axis=0)
    centre = jnp.concatenate([zeros, omega, zeros, zeros] * 2, axis=0)
    first_row = iota((32, 128), 0) == 0
    last_row = iota((32, 128), 0) == 31

    for c in range(CAP):
        pooled[pl.ds(PAD + c * 384, 384), :] = dot(vel[pl.ds(c * 384, 384), :], pool)

    def rows_at(c, i):
        base = PAD + (c * 3 + i) * 128
        return base, [pooled[pl.ds(base + j, 32, stride=4), :] for j in range(4)]

    normals = []
    for c in range(CAP):
        centres = []
        for i in range(3):
            row = rows_at(c, i)[1]
            centres.append(jnp.concatenate(split((row[0] + row[1] + row[2] + row[3]) * SMALL), axis=1))
        normals.append(dot(jnp.concatenate(centres, axis=0), centre))

    def rows_of(block, channel):
        return table[block, channel * 32 : channel * 32 + 32, :].astype(jnp.float32)

    def fold(value):
        return value.reshape(4, 8, 256).sum(0)

    counts = jnp.concatenate([count_vec[...], count_vec[...]], axis=1)
    final = sum(jnp.where(counts == c + 1, 1.0, 0.0) * normals[c] for c in range(CAP))
    edges = (jnp.where(odd, final, normals[0]), jnp.where(odd, normals[0], final))
    found = ([], [])
    for block in range(BLOCKS):
        parts = [jnp.zeros((8, 256), jnp.float32)] * 2
        for i in range(3):
            rows = rows_of(block, 3 * i + 2)
            parts = [part + fold(edge[i * 32 : i * 32 + 32] * rows) for part, edge in zip(parts, edges)]
        for part, rows in zip(parts, found):
            rows.append(jnp.sum(part, axis=0, keepdims=True))
    out[8:16, :] = jnp.concatenate(found[0], axis=0)
    out[16:24, :] = jnp.concatenate(found[1], axis=0)

    wall = dot(shear[...], pool) * SMALL
    first = jnp.broadcast_to(jnp.sum(wall[0:4], axis=0, keepdims=True), (8, 128))
    second = jnp.broadcast_to(jnp.sum(wall[4:8], axis=0, keepdims=True), (8, 128))
    low = jnp.where(group == 0, pltpu.roll(first, 96, 1), jnp.where(group == 1, second, 0.0))
    out[24:32, :] = jnp.concatenate([low, low], axis=1)

    for copy in copies:
        copy.wait()
    count = count_in[0, 0]

    third = iota((3, 128), 1) // 32
    taps = {}
    for i in range(3):
        for q in range(2):
            rows = taps_in[i, q] * SMALL
            rows = [jnp.broadcast_to(rows[:, b : b + 1], (3, 128)) for b in range(3)]
            rows = jnp.where(third == 0, rows[0], jnp.where(third == 1, rows[1], jnp.where(third == 2, rows[2], 0.0)))
            for a in range(3):
                taps[i, q, a] = jnp.broadcast_to(rows[a : a + 1], (8, 128))

    planes = []
    for c in range(CAP):
        feats = []
        for i in range(3):
            base, row = rows_at(c, i)
            before = jnp.where(first_row, 0.0, pooled[pl.ds(base - 1, 32, stride=4), :])
            after = jnp.where(last_row, 0.0, pooled[pl.ds(base + 4, 32, stride=4), :])
            inside = row[1] + row[2]
            head = row[0] + inside
            window = (before + head, head + row[3], inside + row[3] + after)
            for q in range(2):
                mixed = sum(
                    (window[a].reshape(4, 8, 128) * taps[i, q, a][None]).reshape(32, 128) for a in range(3)
                )
                folded = mixed + pltpu.roll(mixed, 96, 1) + pltpu.roll(mixed, 64, 1)
                feats.append(folded.astype(jnp.bfloat16))
        planes.append(dot(jnp.concatenate(feats, axis=0), spread))

    total = jnp.zeros((8, 256), jnp.float32)
    for c in range(CAP):
        alive = jnp.where(c < count, 1.0, 0.0)
        part = jnp.zeros((8, 256), jnp.float32)
        for i in range(3):
            for q in range(2):
                at = (i * 2 + q) * 32
                part += fold(planes[c][at : at + 32] * rows_of(blocks[0, c], 3 * i + q))
            weight = None
            if c:
                weight = spans[0, c - 1] * rows_of(blocks[0, c - 1], 3 * i + 2)
            if c + 1 < CAP:
                span = jnp.where(c + 1 < count, spans[0, c + 1], 0.0)
                down = span * rows_of(blocks[0, c + 1], 3 * i + 2)
                weight = -down if weight is None else weight - down
            part += fold(normals[c][i * 32 : i * 32 + 32] * weight)
        total += alive * part
    out[0:8, :] = total


def send_kernel(part, partner, out):
    odd = lax.axis_index("core") == 1
    tile = partner[...]
    row = iota((8, 128), 0)

    def spread(at):
        return jnp.broadcast_to(tile[at : at + 1], (8, 128))

    span = jnp.where(odd, spread(2), -spread(0))
    block = jnp.where(odd, spread(3), spread(1)).astype(jnp.int32)
    weight = jnp.where(row == block, span, 0.0)
    near = part[16:24, :] * jnp.concatenate([weight, weight], axis=1)
    coef = jnp.sum(part[0:8, :] + near, axis=0, keepdims=True)
    coef = jnp.broadcast_to(coef, (8, 256))

    def pair(value):
        high = value.astype(jnp.bfloat16).astype(jnp.float32)
        return high, value - high

    high, low = pair(coef)
    wall, wall_low = pair(part[24:32, :128])
    wall = wall + pltpu.roll(wall_low, 64, 1)
    far, far_low = pair(jnp.where(odd, -spread(0), spread(2)))
    told = jnp.where(odd, spread(1), spread(3))
    picks = (high[:, :128], high[:, 128:], low[:, :128], low[:, 128:], wall, far, far_low, told)
    small = picks[-1]
    for at in range(7):
        small = jnp.where(row == at, picks[at], small)
    outer = part[8:16, :]
    whole = jnp.concatenate([outer[:, :128], outer[:, 128:], small], axis=0).astype(jnp.bfloat16)
    for copy_at in range(out.shape[0]):
        out[copy_at] = whole


def merge_kernel(rows, out, wide):
    odd = lax.axis_index("core") == 1
    chips = rows.shape[0] // SENT
    wide[...] = rows[...].astype(jnp.float32)

    def every(at):
        return wide[pl.ds(16 + at, chips, stride=SENT), :]

    low = jnp.sum(every(0) + every(2), axis=0, keepdims=True)
    high = jnp.sum(every(1) + every(3), axis=0, keepdims=True)
    wall = every(4)
    wall = wall + pltpu.roll(wall, 64, 1)
    sub = iota((8, 128), 0)
    reach = [jnp.zeros((8, 128), jnp.float32)] * 2
    for j in range(chips):
        span = wide[SENT * j + 21 : SENT * j + 22, :] + wide[SENT * j + 22 : SENT * j + 23, :]
        block = jnp.broadcast_to(wide[SENT * j + 23 : SENT * j + 24, :], (8, 128)).astype(jnp.int32)
        weight = jnp.where(sub == block, jnp.broadcast_to(span, (8, 128)), 0.0)
        before = wide[pl.ds(SENT * (j - 1), 16), :] if j > 0 else jnp.zeros((16, 128), jnp.float32)
        after = wide[pl.ds(SENT * (j + 1), 16), :] if j + 1 < chips else jnp.zeros((16, 128), jnp.float32)
        held = jnp.where(odd, before, after)
        reach = [reach[h] + weight * held[8 * h : 8 * h + 8] for h in range(2)]
    low = low + jnp.sum(reach[0], axis=0, keepdims=True)
    high = high + jnp.sum(reach[1], axis=0, keepdims=True)
    left = iota((8, 128), 1) < 64
    wide[0:chips, :] = wall
    wall = jnp.where(left, wide[pl.ds(0, 8, stride=2), :], wide[pl.ds(1, 8, stride=2), :])
    low = jnp.broadcast_to(low, (8, 128))
    high = jnp.broadcast_to(high, (8, 128))
    low_top = low.astype(jnp.bfloat16).astype(jnp.float32)
    high_top = high.astype(jnp.bfloat16).astype(jnp.float32)
    wall_top = wall.astype(jnp.bfloat16).astype(jnp.float32)
    small = jnp.where(sub == 0, low_top, jnp.where(sub == 1, high_top, jnp.where(sub == 2, low - low_top, jnp.where(sub == 3, high - high_top, 0.0))))
    whole = jnp.concatenate([wall_top, wall - wall_top, small], axis=0).astype(jnp.bfloat16)
    for copy_at in range(out.shape[0]):
        out[copy_at] = whole


def finish_kernel(rows, sketch, gram, wide):
    wide[...] = rows[...].astype(jnp.float32)

    def across(at):
        return wide[pl.ds(at, 16, stride=2 * SENT), :]

    def both(at):
        return across(at) + across(at + 2) + across(at + SENT) + across(at + SENT + 2)

    coef = jnp.concatenate([both(16), both(17)], axis=1)
    coef_high, coef_low = split(coef)
    walls = [
        jnp.concatenate([across(at), across(at + 8)], axis=0).astype(jnp.bfloat16)
        for at in [SENT * core + r for core in range(2) for r in range(8)]
    ]
    wall = jnp.concatenate(walls, axis=1)
    product = lax.dot_general(wall, wall, (((1,), (1,)), ((), ())), preferred_element_type=jnp.float32)
    product = product[0:16] + product[16:32]
    inner = product[:, 0:16] + product[:, 16:32]
    inner_high, inner_low = split(inner)
    right = dot(inner_high, coef_high) + dot(inner_low, coef_high) + dot(inner_high, coef_low)
    right_high, right_low = split(right * (1.0 / 2048.0))
    left = jnp.concatenate([coef_high, coef_low, coef_high], axis=0)
    gram[...] = lax.dot_general(
        left,
        jnp.concatenate([right_high, right_high, right_low], axis=0),
        OVER_ROWS,
        preferred_element_type=jnp.float32,
    )
    core, chip, snap = lax.axis_index("core"), lax.axis_index("z"), lax.axis_index("snap")
    row_at = core * 8 + lax.shift_right_logical(chip, 1)
    mine = jnp.zeros((16, 128), jnp.float32)
    for c in range(2):
        for r in range(8):
            at = SENT * c + r
            mine = jnp.where(row_at == c * 8 + r, across(at) + across(at + 8), mine)
    target = iota((16, 128), 1) - (chip & 1) * 64 - 2 * snap
    for m in range(2):
        for x in range(2):
            column = jnp.sum(jnp.where(target == 32 * m + x, mine, 0.0), axis=1, keepdims=True)
            sketch[m, 0, x : x + 1, :] = jnp.sum(column * coef, axis=0, keepdims=True)


def per_device(velocity, plane_count, inv_span, kernels, omega_block, omega_table, omega_stream, wall_shear):
    f32, bf16 = jnp.float32, jnp.bfloat16
    chips, snaps = lax.axis_size("z"), lax.axis_size("snap")
    count = jnp.broadcast_to(plane_count.reshape(1, 1), (1, 128))
    tile = jax.ShapeDtypeStruct((8, 128), f32)
    base = call(blank_kernel, "blank", tile, [], cost=LONG)()
    own = call(pack_kernel, "pack", tile, [VMEM] * 4, cost=LONG)(
        count, inv_span, omega_block, base
    )
    partner = lax.ppermute(own, "core", [(0, 1), (1, 0)])
    part = call(
        project_kernel,
        "project",
        jax.ShapeDtypeStruct((32, 256), f32),
        [VMEM] * 8,
        [
            pltpu.VMEM((ROWS + 2 * PAD, 128), f32),
            pltpu.SMEM((1, 128), jnp.int32),
            pltpu.SMEM((1, CAP), f32),
            pltpu.SMEM((1, CAP), jnp.int32),
            pltpu.SemaphoreType.DMA((3,)),
        ],
        cost=LONG,
        params=SPREAD,
    )(
        count,
        inv_span,
        omega_block,
        kernels,
        velocity.reshape(ROWS, 128),
        omega_table.reshape(BLOCKS, 288, 256),
        omega_stream,
        wall_shear.reshape(8, 128),
    )
    sent = call(send_kernel, "send", jax.ShapeDtypeStruct((chips, SENT, 128), bf16), [VMEM] * 2)(
        part, partner
    )
    got = lax.all_to_all(sent, "z", 0, 0, tiled=True).reshape(chips * SENT, 128)
    sent = call(
        merge_kernel,
        "merge",
        jax.ShapeDtypeStruct((snaps * 2, SENT, 128), bf16),
        [VMEM],
        [pltpu.VMEM((chips * SENT, 128), f32)],
    )(got)
    got = lax.all_to_all(sent, ("snap", "core"), 0, 0, tiled=True).reshape(snaps * 2 * SENT, 128)
    return call(
        finish_kernel,
        "finish",
        (jax.ShapeDtypeStruct((2, 1, 2, 256), f32), jax.ShapeDtypeStruct((256, 256), f32)),
        [VMEM],
        [pltpu.VMEM((snaps * 2 * SENT, 128), f32)],
    )(got)


def solution(mesh):
    chips = mesh.shape["plane"] // 2
    fine = Mesh(mesh.devices.reshape(mesh.shape["snap"], chips, 2), ("snap", "z", "core"))
    plane = ("z", "core")
    return jax.shard_map(
        per_device,
        mesh=fine,
        in_specs=(
            P("snap", plane, None, None, None),
            P(plane),
            P(plane, None),
            P(),
            P(plane, None),
            P(),
            P(),
            P("snap", None, plane, None),
        ),
        out_specs=(P(None, plane, "snap", None), P()),
        check_vma=False,
    )
```

```python
import jax
import jax.numpy as jnp
from jax import lax
from jax.experimental import pallas as pl
from jax.experimental.pallas import tpu as pltpu
from jax.sharding import Mesh, PartitionSpec as P

CAP = 4
BLOCKS = 8
ROWS = 1536
PAD = 8
SENT = 24
STEP = 3
SMALL = 1.0 / 16.0
LONG = pl.CostEstimate(flops=10**10, bytes_accessed=10**7, transcendentals=0)
GRANT = pltpu.CompilerParams(vmem_limit_bytes=8 << 20)
SPREAD = pltpu.CompilerParams(vmem_limit_bytes=8 << 20)
VMEM = pl.BlockSpec(memory_space=pltpu.VMEM)
OVER_ROWS = (((0,), (0,)), ((), ()))


def iota(shape, dim):
    return lax.broadcasted_iota(jnp.int32, shape, dim)


def ring(chips):
    return [STEP * place % chips for place in range(chips)]


def split(value):
    high = value.astype(jnp.bfloat16)
    low = (value - high.astype(jnp.float32)).astype(jnp.bfloat16)
    return high, low


def dot(left, right):
    return jnp.dot(left, right, preferred_element_type=jnp.float32)


def call(kernel, name, out, ins, scratch=(), cost=None, params=GRANT):
    return pl.pallas_call(
        kernel,
        out_shape=out,
        in_specs=ins,
        out_specs=jax.tree.map(lambda _: VMEM, out),
        scratch_shapes=list(scratch),
        compiler_params=params,
        cost_estimate=cost,
        name=name,
    )


def blank_kernel(out):
    out[...] = jnp.zeros((8, 128), jnp.float32)


def pack_kernel(count, spans, blocks, base, out):
    row = iota((8, 128), 0)
    last = iota((1, CAP), 1) == count[:, 0:CAP] - 1
    marks = blocks[...].astype(jnp.float32)
    tile = base[...]
    for at, values in ((0, spans[...]), (1, marks)):
        final = jnp.sum(jnp.where(last, values, 0.0), axis=1, keepdims=True)
        tile = jnp.where(row == at, jnp.broadcast_to(values[:, 0:1], (8, 128)), tile)
        tile = jnp.where(row == at + 2, jnp.broadcast_to(final, (8, 128)), tile)
    out[...] = tile


def project_kernel(
    count_vec, spans_vec, blocks_vec, taps_in, vel, table, stream, shear, out, pooled, count_in, spans, blocks, sems
):
    pairs = ((count_vec, count_in), (spans_vec, spans), (blocks_vec, blocks))
    copies = [pltpu.make_async_copy(source, target, sems.at[at]) for at, (source, target) in enumerate(pairs)]
    for copy in copies:
        copy.start()
    odd = lax.axis_index("core") == 1

    lane = iota((128, 128), 1)
    gap = iota((128, 128), 0) - 4 * (lane % 32) - lane // 32 + 1
    pool = jnp.where((gap >= 0) & (gap < 4) & (lane < 96), 1.0, 0.0).astype(jnp.bfloat16)
    group = iota((8, 128), 1) // 32

    zeros = jnp.zeros((32, 256), jnp.bfloat16)
    omega = stream[...]
    spread = jnp.concatenate([omega, zeros, zeros, zeros], axis=0)
    centre = jnp.concatenate([zeros, omega, zeros, zeros] * 2, axis=0)
    first_row = iota((32, 128), 0) == 0
    last_row = iota((32, 128), 0) == 31

    for c in range(CAP):
        pooled[pl.ds(PAD + c * 384, 384), :] = dot(vel[pl.ds(c * 384, 384), :], pool)

    def rows_at(c, i):
        base = PAD + (c * 3 + i) * 128
        return base, [pooled[pl.ds(base + j, 32, stride=4), :] for j in range(4)]

    normals = []
    for c in range(CAP):
        centres = []
        for i in range(3):
            row = rows_at(c, i)[1]
            centres.append(jnp.concatenate(split((row[0] + row[1] + row[2] + row[3]) * SMALL), axis=1))
        normals.append(dot(jnp.concatenate(centres, axis=0), centre))

    def rows_of(block, channel):
        return table[block, channel * 32 : channel * 32 + 32, :].astype(jnp.float32)

    def fold(value):
        return value.reshape(4, 8, 256).sum(0)

    counts = jnp.concatenate([count_vec[...], count_vec[...]], axis=1)
    final = sum(jnp.where(counts == c + 1, 1.0, 0.0) * normals[c] for c in range(CAP))
    edges = (jnp.where(odd, final, normals[0]), jnp.where(odd, normals[0], final))
    found = ([], [])
    for block in range(BLOCKS):
        parts = [jnp.zeros((8, 256), jnp.float32)] * 2
        for i in range(3):
            rows = rows_of(block, 3 * i + 2)
            parts = [part + fold(edge[i * 32 : i * 32 + 32] * rows) for part, edge in zip(parts, edges)]
        for part, rows in zip(parts, found):
            rows.append(jnp.sum(part, axis=0, keepdims=True))
    out[8:16, :] = jnp.concatenate(found[0], axis=0)
    out[16:24, :] = jnp.concatenate(found[1], axis=0)

    wall = dot(shear[...], pool) * SMALL
    first = jnp.broadcast_to(jnp.sum(wall[0:4], axis=0, keepdims=True), (8, 128))
    second = jnp.broadcast_to(jnp.sum(wall[4:8], axis=0, keepdims=True), (8, 128))
    low = jnp.where(group == 0, pltpu.roll(first, 96, 1), jnp.where(group == 1, second, 0.0))
    out[24:32, :] = jnp.concatenate([low, low], axis=1)

    for copy in copies:
        copy.wait()
    count = count_in[0, 0]

    third = iota((3, 128), 1) // 32
    taps = {}
    for i in range(3):
        for q in range(2):
            rows = taps_in[i, q] * SMALL
            rows = [jnp.broadcast_to(rows[:, b : b + 1], (3, 128)) for b in range(3)]
            rows = jnp.where(third == 0, rows[0], jnp.where(third == 1, rows[1], jnp.where(third == 2, rows[2], 0.0)))
            for a in range(3):
                taps[i, q, a] = jnp.broadcast_to(rows[a : a + 1], (8, 128))

    planes = []
    for c in range(CAP):
        feats = []
        for i in range(3):
            base, row = rows_at(c, i)
            before = jnp.where(first_row, 0.0, pooled[pl.ds(base - 1, 32, stride=4), :])
            after = jnp.where(last_row, 0.0, pooled[pl.ds(base + 4, 32, stride=4), :])
            inside = row[1] + row[2]
            head = row[0] + inside
            window = (before + head, head + row[3], inside + row[3] + after)
            for q in range(2):
                mixed = sum(
                    (window[a].reshape(4, 8, 128) * taps[i, q, a][None]).reshape(32, 128) for a in range(3)
                )
                folded = mixed + pltpu.roll(mixed, 96, 1) + pltpu.roll(mixed, 64, 1)
                feats.append(folded.astype(jnp.bfloat16))
        planes.append(dot(jnp.concatenate(feats, axis=0), spread))

    total = jnp.zeros((8, 256), jnp.float32)
    for c in range(CAP):
        alive = jnp.where(c < count, 1.0, 0.0)
        part = jnp.zeros((8, 256), jnp.float32)
        for i in range(3):
            for q in range(2):
                at = (i * 2 + q) * 32
                part += fold(planes[c][at : at + 32] * rows_of(blocks[0, c], 3 * i + q))
            weight = None
            if c:
                weight = spans[0, c - 1] * rows_of(blocks[0, c - 1], 3 * i + 2)
            if c + 1 < CAP:
                span = jnp.where(c + 1 < count, spans[0, c + 1], 0.0)
                down = span * rows_of(blocks[0, c + 1], 3 * i + 2)
                weight = -down if weight is None else weight - down
            part += fold(normals[c][i * 32 : i * 32 + 32] * weight)
        total += alive * part
    out[0:8, :] = total


def send_kernel(part, partner, out):
    odd = lax.axis_index("core") == 1
    tile = partner[...]
    row = iota((8, 128), 0)

    def spread(at):
        return jnp.broadcast_to(tile[at : at + 1], (8, 128))

    span = jnp.where(odd, spread(2), -spread(0))
    block = jnp.where(odd, spread(3), spread(1)).astype(jnp.int32)
    weight = jnp.where(row == block, span, 0.0)
    near = part[16:24, :] * jnp.concatenate([weight, weight], axis=1)
    coef = jnp.sum(part[0:8, :] + near, axis=0, keepdims=True)
    coef = jnp.broadcast_to(coef, (8, 256))

    def pair(value):
        high = value.astype(jnp.bfloat16).astype(jnp.float32)
        return high, value - high

    high, low = pair(coef)
    wall, wall_low = pair(part[24:32, :128])
    wall = wall + pltpu.roll(wall_low, 64, 1)
    far, far_low = pair(jnp.where(odd, -spread(0), spread(2)))
    told = jnp.where(odd, spread(1), spread(3))
    picks = (high[:, :128], high[:, 128:], low[:, :128], low[:, 128:], wall, far, far_low, told)
    small = picks[-1]
    for at in range(7):
        small = jnp.where(row == at, picks[at], small)
    outer = part[8:16, :]
    whole = jnp.concatenate([outer[:, :128], outer[:, 128:], small], axis=0).astype(jnp.bfloat16)
    for copy_at in range(out.shape[0]):
        out[copy_at] = whole


def merge_kernel(rows, out, wide):
    odd = lax.axis_index("core") == 1
    chips = rows.shape[0] // SENT
    wide[...] = rows[...].astype(jnp.float32)

    def every(at):
        return wide[pl.ds(16 + at, chips, stride=SENT), :]

    low = jnp.sum(every(0) + every(2), axis=0, keepdims=True)
    high = jnp.sum(every(1) + every(3), axis=0, keepdims=True)
    wall = every(4)
    wall = wall + pltpu.roll(wall, 64, 1)
    sub = iota((8, 128), 0)
    reach = [jnp.zeros((8, 128), jnp.float32)] * 2
    order = ring(chips)
    for j in range(chips):
        at = SENT * order.index(j)
        span = wide[at + 21 : at + 22, :] + wide[at + 22 : at + 23, :]
        block = jnp.broadcast_to(wide[at + 23 : at + 24, :], (8, 128)).astype(jnp.int32)
        weight = jnp.where(sub == block, jnp.broadcast_to(span, (8, 128)), 0.0)
        before = wide[pl.ds(SENT * order.index(j - 1), 16), :] if j > 0 else jnp.zeros((16, 128), jnp.float32)
        after = wide[pl.ds(SENT * order.index(j + 1), 16), :] if j + 1 < chips else jnp.zeros((16, 128), jnp.float32)
        held = jnp.where(odd, before, after)
        reach = [reach[h] + weight * held[8 * h : 8 * h + 8] for h in range(2)]
    low = low + jnp.sum(reach[0], axis=0, keepdims=True)
    high = high + jnp.sum(reach[1], axis=0, keepdims=True)
    left = iota((8, 128), 1) < 64
    wide[0:chips, :] = wall
    wall = jnp.where(left, wide[pl.ds(0, 8, stride=2), :], wide[pl.ds(1, 8, stride=2), :])
    low = jnp.broadcast_to(low, (8, 128))
    high = jnp.broadcast_to(high, (8, 128))
    low_top = low.astype(jnp.bfloat16).astype(jnp.float32)
    high_top = high.astype(jnp.bfloat16).astype(jnp.float32)
    wall_top = wall.astype(jnp.bfloat16).astype(jnp.float32)
    small = jnp.where(sub == 0, low_top, jnp.where(sub == 1, high_top, jnp.where(sub == 2, low - low_top, jnp.where(sub == 3, high - high_top, 0.0))))
    whole = jnp.concatenate([wall_top, wall - wall_top, small], axis=0).astype(jnp.bfloat16)
    for copy_at in range(out.shape[0]):
        out[copy_at] = whole


def finish_kernel(rows, sketch, gram, wide):
    wide[...] = rows[...].astype(jnp.float32)

    def across(core, at):
        return wide[pl.ds(16 * SENT * core + at, 16, stride=SENT), :]

    def both(at):
        return across(0, at) + across(0, at + 2) + across(1, at) + across(1, at + 2)

    coef = jnp.concatenate([both(16), both(17)], axis=1)
    coef_high, coef_low = split(coef)
    walls = [
        jnp.concatenate([across(core, r), across(core, r + 8)], axis=0).astype(jnp.bfloat16)
        for core in range(2)
        for r in range(8)
    ]
    wall = jnp.concatenate(walls, axis=1)
    product = lax.dot_general(wall, wall, (((1,), (1,)), ((), ())), preferred_element_type=jnp.float32)
    product = product[0:16] + product[16:32]
    inner = product[:, 0:16] + product[:, 16:32]
    inner_high, inner_low = split(inner)
    right = dot(inner_high, coef_high) + dot(inner_low, coef_high) + dot(inner_high, coef_low)
    right_high, right_low = split(right * (1.0 / 2048.0))
    left = jnp.concatenate([coef_high, coef_low, coef_high], axis=0)
    gram[...] = lax.dot_general(
        left,
        jnp.concatenate([right_high, right_high, right_low], axis=0),
        OVER_ROWS,
        preferred_element_type=jnp.float32,
    )
    core, chip, snap = lax.axis_index("core"), lax.axis_index("z"), lax.axis_index("snap")
    place = lax.rem(chip * pow(STEP, -1, 16), 16)
    row_at = core * 8 + lax.shift_right_logical(place, 1)
    mine = jnp.zeros((16, 128), jnp.float32)
    for c in range(2):
        for r in range(8):
            mine = jnp.where(row_at == c * 8 + r, across(c, r) + across(c, r + 8), mine)
    target = iota((16, 128), 1) - (place & 1) * 64 - 2 * snap
    for m in range(2):
        for x in range(2):
            column = jnp.sum(jnp.where(target == 32 * m + x, mine, 0.0), axis=1, keepdims=True)
            sketch[m, 0, x : x + 1, :] = jnp.sum(column * coef, axis=0, keepdims=True)


def per_device(velocity, plane_count, inv_span, kernels, omega_block, omega_table, omega_stream, wall_shear):
    f32, bf16 = jnp.float32, jnp.bfloat16
    chips, snaps = lax.axis_size("z"), lax.axis_size("snap")
    count = jnp.broadcast_to(plane_count.reshape(1, 1), (1, 128))
    tile = jax.ShapeDtypeStruct((8, 128), f32)
    base = call(blank_kernel, "blank", tile, [], cost=LONG)()
    own = call(pack_kernel, "pack", tile, [VMEM] * 4, cost=LONG)(
        count, inv_span, omega_block, base
    )
    partner = lax.ppermute(own, "core", [(0, 1), (1, 0)])
    part = call(
        project_kernel,
        "project",
        jax.ShapeDtypeStruct((32, 256), f32),
        [VMEM] * 8,
        [
            pltpu.VMEM((ROWS + 2 * PAD, 128), f32),
            pltpu.SMEM((1, 128), jnp.int32),
            pltpu.SMEM((1, CAP), f32),
            pltpu.SMEM((1, CAP), jnp.int32),
            pltpu.SemaphoreType.DMA((3,)),
        ],
        cost=LONG,
        params=SPREAD,
    )(
        count,
        inv_span,
        omega_block,
        kernels,
        velocity.reshape(ROWS, 128),
        omega_table.reshape(BLOCKS, 288, 256),
        omega_stream,
        wall_shear.reshape(8, 128),
    )
    sent = call(send_kernel, "send", jax.ShapeDtypeStruct((chips, SENT, 128), bf16), [VMEM] * 2)(
        part, partner
    )
    got = lax.all_to_all(sent, "z", 0, 0, tiled=True, axis_index_groups=[ring(chips)]).reshape(chips * SENT, 128)
    sent = call(
        merge_kernel,
        "merge",
        jax.ShapeDtypeStruct((snaps * 2, SENT, 128), bf16),
        [VMEM],
        [pltpu.VMEM((chips * SENT, 128), f32)],
    )(got)
    got = lax.all_to_all(sent, ("core", "snap"), 0, 0, tiled=True).reshape(snaps * 2 * SENT, 128)
    return call(
        finish_kernel,
        "finish",
        (jax.ShapeDtypeStruct((2, 1, 2, 256), f32), jax.ShapeDtypeStruct((256, 256), f32)),
        [VMEM],
        [pltpu.VMEM((snaps * 2 * SENT, 128), f32)],
    )(got)


def solution(mesh):
    chips = mesh.shape["plane"] // 2
    fine = Mesh(mesh.devices.reshape(mesh.shape["snap"], chips, 2), ("snap", "z", "core"))
    plane = ("z", "core")
    return jax.shard_map(
        per_device,
        mesh=fine,
        in_specs=(
            P("snap", plane, None, None, None),
            P(plane),
            P(plane, None),
            P(),
            P(plane, None),
            P(),
            P(),
            P("snap", None, plane, None),
        ),
        out_specs=(P(None, plane, "snap", None), P()),
        check_vma=False,
    )
```

```python
import jax
import jax.numpy as jnp
from jax import lax
from jax.experimental import pallas as pl
from jax.experimental.pallas import tpu as pltpu
from jax.sharding import Mesh, PartitionSpec as P

CAP = 4
BLOCKS = 8
ROWS = 1536
PAD = 8
SENT = 24
STEP = 3
SMALL = 1.0 / 16.0
LONG = pl.CostEstimate(flops=10**10, bytes_accessed=10**7, transcendentals=0)
GRANT = pltpu.CompilerParams(vmem_limit_bytes=8 << 20)
SPREAD = pltpu.CompilerParams(vmem_limit_bytes=8 << 20)
VMEM = pl.BlockSpec(memory_space=pltpu.VMEM)
OVER_ROWS = (((0,), (0,)), ((), ()))


def iota(shape, dim):
    return lax.broadcasted_iota(jnp.int32, shape, dim)


def ring(chips):
    return [STEP * place % chips for place in range(chips)]


def split(value):
    high = value.astype(jnp.bfloat16)
    low = (value - high.astype(jnp.float32)).astype(jnp.bfloat16)
    return high, low


def dot(left, right):
    return jnp.dot(left, right, preferred_element_type=jnp.float32)


def call(kernel, name, out, ins, scratch=(), cost=None, params=GRANT):
    return pl.pallas_call(
        kernel,
        out_shape=out,
        in_specs=ins,
        out_specs=jax.tree.map(lambda _: VMEM, out),
        scratch_shapes=list(scratch),
        compiler_params=params,
        cost_estimate=cost,
        name=name,
    )


def blank_kernel(out):
    out[...] = jnp.zeros((8, 128), jnp.float32)


def pack_kernel(count, spans, blocks, base, out):
    row = iota((8, 128), 0)
    last = iota((1, CAP), 1) == count[:, 0:CAP] - 1
    marks = blocks[...].astype(jnp.float32)
    tile = base[...]
    for at, values in ((0, spans[...]), (1, marks)):
        final = jnp.sum(jnp.where(last, values, 0.0), axis=1, keepdims=True)
        tile = jnp.where(row == at, jnp.broadcast_to(values[:, 0:1], (8, 128)), tile)
        tile = jnp.where(row == at + 2, jnp.broadcast_to(final, (8, 128)), tile)
    out[...] = tile


def project_kernel(
    count_vec, spans_vec, blocks_vec, taps_in, vel, table, stream, shear, out, pooled, count_in, spans, blocks, sems
):
    pairs = ((count_vec, count_in), (spans_vec, spans), (blocks_vec, blocks))
    copies = [pltpu.make_async_copy(source, target, sems.at[at]) for at, (source, target) in enumerate(pairs)]
    for copy in copies:
        copy.start()
    odd = lax.axis_index("core") == 1

    lane = iota((128, 128), 1)
    gap = iota((128, 128), 0) - 4 * (lane % 32) - lane // 32 + 1
    pool = jnp.where((gap >= 0) & (gap < 4) & (lane < 96), 1.0, 0.0).astype(jnp.bfloat16)
    group = iota((8, 128), 1) // 32

    zeros = jnp.zeros((32, 256), jnp.bfloat16)
    omega = stream[...]
    spread = jnp.concatenate([omega, zeros, zeros, zeros], axis=0)
    centre = jnp.concatenate([zeros, omega, zeros, zeros] * 2, axis=0)
    first_row = iota((32, 128), 0) == 0
    last_row = iota((32, 128), 0) == 31

    for c in range(CAP):
        pooled[pl.ds(PAD + c * 384, 384), :] = dot(vel[pl.ds(c * 384, 384), :], pool)

    def rows_at(c, i):
        base = PAD + (c * 3 + i) * 128
        return base, [pooled[pl.ds(base + j, 32, stride=4), :] for j in range(4)]

    normals = []
    for c in range(CAP):
        centres = []
        for i in range(3):
            row = rows_at(c, i)[1]
            centres.append(jnp.concatenate(split((row[0] + row[1] + row[2] + row[3]) * SMALL), axis=1))
        normals.append(dot(jnp.concatenate(centres, axis=0), centre))

    def rows_of(block, channel):
        return table[block, channel * 32 : channel * 32 + 32, :].astype(jnp.float32)

    def fold(value):
        return value.reshape(4, 8, 256).sum(0)

    counts = jnp.concatenate([count_vec[...], count_vec[...]], axis=1)
    final = sum(jnp.where(counts == c + 1, 1.0, 0.0) * normals[c] for c in range(CAP))
    edges = (jnp.where(odd, final, normals[0]), jnp.where(odd, normals[0], final))
    found = ([], [])
    for block in range(BLOCKS):
        parts = [jnp.zeros((8, 256), jnp.float32)] * 2
        for i in range(3):
            rows = rows_of(block, 3 * i + 2)
            parts = [part + fold(edge[i * 32 : i * 32 + 32] * rows) for part, edge in zip(parts, edges)]
        for part, rows in zip(parts, found):
            rows.append(jnp.sum(part, axis=0, keepdims=True))
    out[8:16, :] = jnp.concatenate(found[0], axis=0)
    out[16:24, :] = jnp.concatenate(found[1], axis=0)

    wall = dot(shear[...], pool) * SMALL
    first = jnp.broadcast_to(jnp.sum(wall[0:4], axis=0, keepdims=True), (8, 128))
    second = jnp.broadcast_to(jnp.sum(wall[4:8], axis=0, keepdims=True), (8, 128))
    low = jnp.where(group == 0, pltpu.roll(first, 96, 1), jnp.where(group == 1, second, 0.0))
    out[24:32, :] = jnp.concatenate([low, low], axis=1)


    third = iota((3, 128), 1) // 32
    taps = {}
    for i in range(3):
        for q in range(2):
            rows = taps_in[i, q] * SMALL
            rows = [jnp.broadcast_to(rows[:, b : b + 1], (3, 128)) for b in range(3)]
            rows = jnp.where(third == 0, rows[0], jnp.where(third == 1, rows[1], jnp.where(third == 2, rows[2], 0.0)))
            for a in range(3):
                taps[i, q, a] = jnp.broadcast_to(rows[a : a + 1], (8, 128))

    planes = []
    for c in range(CAP):
        feats = []
        for i in range(3):
            base, row = rows_at(c, i)
            before = jnp.where(first_row, 0.0, pooled[pl.ds(base - 1, 32, stride=4), :])
            after = jnp.where(last_row, 0.0, pooled[pl.ds(base + 4, 32, stride=4), :])
            inside = row[1] + row[2]
            head = row[0] + inside
            window = (before + head, head + row[3], inside + row[3] + after)
            for q in range(2):
                mixed = sum(
                    (window[a].reshape(4, 8, 128) * taps[i, q, a][None]).reshape(32, 128) for a in range(3)
                )
                folded = mixed + pltpu.roll(mixed, 96, 1) + pltpu.roll(mixed, 64, 1)
                feats.append(folded.astype(jnp.bfloat16))
        planes.append(dot(jnp.concatenate(feats, axis=0), spread))

    for copy in copies:
        copy.wait()
    count = count_in[0, 0]
    total = jnp.zeros((8, 256), jnp.float32)
    for c in range(CAP):
        alive = jnp.where(c < count, 1.0, 0.0)
        part = jnp.zeros((8, 256), jnp.float32)
        for i in range(3):
            for q in range(2):
                at = (i * 2 + q) * 32
                part += fold(planes[c][at : at + 32] * rows_of(blocks[0, c], 3 * i + q))
            weight = None
            if c:
                weight = spans[0, c - 1] * rows_of(blocks[0, c - 1], 3 * i + 2)
            if c + 1 < CAP:
                span = jnp.where(c + 1 < count, spans[0, c + 1], 0.0)
                down = span * rows_of(blocks[0, c + 1], 3 * i + 2)
                weight = -down if weight is None else weight - down
            part += fold(normals[c][i * 32 : i * 32 + 32] * weight)
        total += alive * part
    out[0:8, :] = total


def send_kernel(part, partner, out):
    odd = lax.axis_index("core") == 1
    tile = partner[...]
    row = iota((8, 128), 0)

    def spread(at):
        return jnp.broadcast_to(tile[at : at + 1], (8, 128))

    span = jnp.where(odd, spread(2), -spread(0))
    block = jnp.where(odd, spread(3), spread(1)).astype(jnp.int32)
    weight = jnp.where(row == block, span, 0.0)
    near = part[16:24, :] * jnp.concatenate([weight, weight], axis=1)
    coef = jnp.sum(part[0:8, :] + near, axis=0, keepdims=True)
    coef = jnp.broadcast_to(coef, (8, 256))

    def pair(value):
        high = value.astype(jnp.bfloat16).astype(jnp.float32)
        return high, value - high

    high, low = pair(coef)
    wall, wall_low = pair(part[24:32, :128])
    wall = wall + pltpu.roll(wall_low, 64, 1)
    far, far_low = pair(jnp.where(odd, -spread(0), spread(2)))
    told = jnp.where(odd, spread(1), spread(3))
    picks = (high[:, :128], high[:, 128:], low[:, :128], low[:, 128:], wall, far, far_low, told)
    small = picks[-1]
    for at in range(7):
        small = jnp.where(row == at, picks[at], small)
    outer = part[8:16, :]
    whole = jnp.concatenate([outer[:, :128], outer[:, 128:], small], axis=0).astype(jnp.bfloat16)
    for copy_at in range(out.shape[0]):
        out[copy_at] = whole


def merge_kernel(rows, out, wide):
    odd = lax.axis_index("core") == 1
    chips = rows.shape[0] // SENT
    wide[...] = rows[...].astype(jnp.float32)

    def every(at):
        return wide[pl.ds(16 + at, chips, stride=SENT), :]

    low = jnp.sum(every(0) + every(2), axis=0, keepdims=True)
    high = jnp.sum(every(1) + every(3), axis=0, keepdims=True)
    wall = every(4)
    wall = wall + pltpu.roll(wall, 64, 1)
    sub = iota((8, 128), 0)
    reach = [jnp.zeros((8, 128), jnp.float32)] * 2
    order = ring(chips)
    for j in range(chips):
        at = SENT * order.index(j)
        span = wide[at + 21 : at + 22, :] + wide[at + 22 : at + 23, :]
        block = jnp.broadcast_to(wide[at + 23 : at + 24, :], (8, 128)).astype(jnp.int32)
        weight = jnp.where(sub == block, jnp.broadcast_to(span, (8, 128)), 0.0)
        before = wide[pl.ds(SENT * order.index(j - 1), 16), :] if j > 0 else jnp.zeros((16, 128), jnp.float32)
        after = wide[pl.ds(SENT * order.index(j + 1), 16), :] if j + 1 < chips else jnp.zeros((16, 128), jnp.float32)
        held = jnp.where(odd, before, after)
        reach = [reach[h] + weight * held[8 * h : 8 * h + 8] for h in range(2)]
    low = low + jnp.sum(reach[0], axis=0, keepdims=True)
    high = high + jnp.sum(reach[1], axis=0, keepdims=True)
    left = iota((8, 128), 1) < 64
    wide[0:chips, :] = wall
    wall = jnp.where(left, wide[pl.ds(0, 8, stride=2), :], wide[pl.ds(1, 8, stride=2), :])
    low = jnp.broadcast_to(low, (8, 128))
    high = jnp.broadcast_to(high, (8, 128))
    low_top = low.astype(jnp.bfloat16).astype(jnp.float32)
    high_top = high.astype(jnp.bfloat16).astype(jnp.float32)
    wall_top = wall.astype(jnp.bfloat16).astype(jnp.float32)
    small = jnp.where(sub == 0, low_top, jnp.where(sub == 1, high_top, jnp.where(sub == 2, low - low_top, jnp.where(sub == 3, high - high_top, 0.0))))
    whole = jnp.concatenate([wall_top, wall - wall_top, small], axis=0).astype(jnp.bfloat16)
    for copy_at in range(out.shape[0]):
        out[copy_at] = whole


def finish_kernel(rows, sketch, gram, wide):
    wide[...] = rows[...].astype(jnp.float32)

    def across(core, at):
        return wide[pl.ds(16 * SENT * core + at, 16, stride=SENT), :]

    def both(at):
        return across(0, at) + across(0, at + 2) + across(1, at) + across(1, at + 2)

    coef = jnp.concatenate([both(16), both(17)], axis=1)
    coef_high, coef_low = split(coef)
    walls = [
        jnp.concatenate([across(core, r), across(core, r + 8)], axis=0).astype(jnp.bfloat16)
        for core in range(2)
        for r in range(8)
    ]
    wall = jnp.concatenate(walls, axis=1)
    product = lax.dot_general(wall, wall, (((1,), (1,)), ((), ())), preferred_element_type=jnp.float32)
    product = product[0:16] + product[16:32]
    inner = product[:, 0:16] + product[:, 16:32]
    inner_high, inner_low = split(inner)
    right = dot(inner_high, coef_high) + dot(inner_low, coef_high) + dot(inner_high, coef_low)
    right_high, right_low = split(right * (1.0 / 2048.0))
    left = jnp.concatenate([coef_high, coef_low, coef_high], axis=0)
    gram[...] = lax.dot_general(
        left,
        jnp.concatenate([right_high, right_high, right_low], axis=0),
        OVER_ROWS,
        preferred_element_type=jnp.float32,
    )
    core, chip, snap = lax.axis_index("core"), lax.axis_index("z"), lax.axis_index("snap")
    place = lax.rem(chip * pow(STEP, -1, 16), 16)
    row_at = core * 8 + lax.shift_right_logical(place, 1)
    mine = jnp.zeros((16, 128), jnp.float32)
    for c in range(2):
        for r in range(8):
            mine = jnp.where(row_at == c * 8 + r, across(c, r) + across(c, r + 8), mine)
    target = iota((16, 128), 1) - (place & 1) * 64 - 2 * snap
    for m in range(2):
        for x in range(2):
            column = jnp.sum(jnp.where(target == 32 * m + x, mine, 0.0), axis=1, keepdims=True)
            sketch[m, 0, x : x + 1, :] = jnp.sum(column * coef, axis=0, keepdims=True)


def per_device(velocity, plane_count, inv_span, kernels, omega_block, omega_table, omega_stream, wall_shear):
    f32, bf16 = jnp.float32, jnp.bfloat16
    chips, snaps = lax.axis_size("z"), lax.axis_size("snap")
    count = jnp.broadcast_to(plane_count.reshape(1, 1), (1, 128))
    tile = jax.ShapeDtypeStruct((8, 128), f32)
    base = call(blank_kernel, "blank", tile, [], cost=LONG)()
    own = call(pack_kernel, "pack", tile, [VMEM] * 4, cost=LONG)(
        count, inv_span, omega_block, base
    )
    partner = lax.ppermute(own, "core", [(0, 1), (1, 0)])
    part = call(
        project_kernel,
        "project",
        jax.ShapeDtypeStruct((32, 256), f32),
        [VMEM] * 8,
        [
            pltpu.VMEM((ROWS + 2 * PAD, 128), f32),
            pltpu.SMEM((1, 128), jnp.int32),
            pltpu.SMEM((1, CAP), f32),
            pltpu.SMEM((1, CAP), jnp.int32),
            pltpu.SemaphoreType.DMA((3,)),
        ],
        cost=LONG,
        params=SPREAD,
    )(
        count,
        inv_span,
        omega_block,
        kernels,
        velocity.reshape(ROWS, 128),
        omega_table.reshape(BLOCKS, 288, 256),
        omega_stream,
        wall_shear.reshape(8, 128),
    )
    sent = call(send_kernel, "send", jax.ShapeDtypeStruct((chips, SENT, 128), bf16), [VMEM] * 2)(
        part, partner
    )
    got = lax.all_to_all(sent, "z", 0, 0, tiled=True, axis_index_groups=[ring(chips)]).reshape(chips * SENT, 128)
    sent = call(
        merge_kernel,
        "merge",
        jax.ShapeDtypeStruct((snaps * 2, SENT, 128), bf16),
        [VMEM],
        [pltpu.VMEM((chips * SENT, 128), f32)],
    )(got)
    got = lax.all_to_all(sent, ("core", "snap"), 0, 0, tiled=True).reshape(snaps * 2 * SENT, 128)
    return call(
        finish_kernel,
        "finish",
        (jax.ShapeDtypeStruct((2, 1, 2, 256), f32), jax.ShapeDtypeStruct((256, 256), f32)),
        [VMEM],
        [pltpu.VMEM((snaps * 2 * SENT, 128), f32)],
    )(got)


def solution(mesh):
    chips = mesh.shape["plane"] // 2
    fine = Mesh(mesh.devices.reshape(mesh.shape["snap"], chips, 2), ("snap", "z", "core"))
    plane = ("z", "core")
    return jax.shard_map(
        per_device,
        mesh=fine,
        in_specs=(
            P("snap", plane, None, None, None),
            P(plane),
            P(plane, None),
            P(),
            P(plane, None),
            P(),
            P(),
            P("snap", None, plane, None),
        ),
        out_specs=(P(None, plane, "snap", None), P()),
        check_vma=False,
    )
```

```python
import jax
import jax.numpy as jnp
from jax import lax
from jax.experimental import pallas as pl
from jax.experimental.pallas import tpu as pltpu
from jax.sharding import Mesh, PartitionSpec as P

CAP = 4
BLOCKS = 8
ROWS = 1536
PAD = 8
SENT = 24
STEP = 13
SMALL = 1.0 / 16.0
LONG = pl.CostEstimate(flops=10**10, bytes_accessed=10**7, transcendentals=0)
GRANT = pltpu.CompilerParams(vmem_limit_bytes=8 << 20)
SPREAD = pltpu.CompilerParams(vmem_limit_bytes=8 << 20)
VMEM = pl.BlockSpec(memory_space=pltpu.VMEM)
OVER_ROWS = (((0,), (0,)), ((), ()))


def iota(shape, dim):
    return lax.broadcasted_iota(jnp.int32, shape, dim)


def ring(chips):
    return [STEP * place % chips for place in range(chips)]


def split(value):
    high = value.astype(jnp.bfloat16)
    low = (value - high.astype(jnp.float32)).astype(jnp.bfloat16)
    return high, low


def dot(left, right):
    return jnp.dot(left, right, preferred_element_type=jnp.float32)


def call(kernel, name, out, ins, scratch=(), cost=None, params=GRANT):
    return pl.pallas_call(
        kernel,
        out_shape=out,
        in_specs=ins,
        out_specs=jax.tree.map(lambda _: VMEM, out),
        scratch_shapes=list(scratch),
        compiler_params=params,
        cost_estimate=cost,
        name=name,
    )


def blank_kernel(out):
    out[...] = jnp.zeros((8, 128), jnp.float32)


def pack_kernel(count, spans, blocks, base, out):
    row = iota((8, 128), 0)
    last = iota((1, CAP), 1) == count[:, 0:CAP] - 1
    marks = blocks[...].astype(jnp.float32)
    tile = base[...]
    for at, values in ((0, spans[...]), (1, marks)):
        final = jnp.sum(jnp.where(last, values, 0.0), axis=1, keepdims=True)
        tile = jnp.where(row == at, jnp.broadcast_to(values[:, 0:1], (8, 128)), tile)
        tile = jnp.where(row == at + 2, jnp.broadcast_to(final, (8, 128)), tile)
    out[...] = tile


def project_kernel(
    count_vec, spans_vec, blocks_vec, taps_in, vel, table, stream, shear, out, pooled, count_in, spans, blocks, sems
):
    pairs = ((count_vec, count_in), (spans_vec, spans), (blocks_vec, blocks))
    copies = [pltpu.make_async_copy(source, target, sems.at[at]) for at, (source, target) in enumerate(pairs)]
    for copy in copies:
        copy.start()
    odd = lax.axis_index("core") == 1

    lane = iota((128, 128), 1)
    gap = iota((128, 128), 0) - 4 * (lane % 32) - lane // 32 + 1
    pool = jnp.where((gap >= 0) & (gap < 4) & (lane < 96), 1.0, 0.0).astype(jnp.bfloat16)
    group = iota((8, 128), 1) // 32

    zeros = jnp.zeros((32, 256), jnp.bfloat16)
    omega = stream[...]
    spread = jnp.concatenate([omega, zeros, zeros, zeros], axis=0)
    centre = jnp.concatenate([zeros, omega, zeros, zeros] * 2, axis=0)
    first_row = iota((32, 128), 0) == 0
    last_row = iota((32, 128), 0) == 31

    for c in range(CAP):
        pooled[pl.ds(PAD + c * 384, 384), :] = dot(vel[pl.ds(c * 384, 384), :], pool)

    def rows_at(c, i):
        base = PAD + (c * 3 + i) * 128
        return base, [pooled[pl.ds(base + j, 32, stride=4), :] for j in range(4)]

    normals = []
    for c in range(CAP):
        centres = []
        for i in range(3):
            row = rows_at(c, i)[1]
            centres.append(jnp.concatenate(split((row[0] + row[1] + row[2] + row[3]) * SMALL), axis=1))
        normals.append(dot(jnp.concatenate(centres, axis=0), centre))

    def rows_of(block, channel):
        return table[block, channel * 32 : channel * 32 + 32, :].astype(jnp.float32)

    def fold(value):
        return value.reshape(4, 8, 256).sum(0)

    counts = jnp.concatenate([count_vec[...], count_vec[...]], axis=1)
    final = sum(jnp.where(counts == c + 1, 1.0, 0.0) * normals[c] for c in range(CAP))
    edges = (jnp.where(odd, final, normals[0]), jnp.where(odd, normals[0], final))
    found = ([], [])
    for block in range(BLOCKS):
        parts = [jnp.zeros((8, 256), jnp.float32)] * 2
        for i in range(3):
            rows = rows_of(block, 3 * i + 2)
            parts = [part + fold(edge[i * 32 : i * 32 + 32] * rows) for part, edge in zip(parts, edges)]
        for part, rows in zip(parts, found):
            rows.append(jnp.sum(part, axis=0, keepdims=True))
    out[8:16, :] = jnp.concatenate(found[0], axis=0)
    out[16:24, :] = jnp.concatenate(found[1], axis=0)

    wall = dot(shear[...], pool) * SMALL
    first = jnp.broadcast_to(jnp.sum(wall[0:4], axis=0, keepdims=True), (8, 128))
    second = jnp.broadcast_to(jnp.sum(wall[4:8], axis=0, keepdims=True), (8, 128))
    low = jnp.where(group == 0, pltpu.roll(first, 96, 1), jnp.where(group == 1, second, 0.0))
    out[24:32, :] = jnp.concatenate([low, low], axis=1)


    third = iota((3, 128), 1) // 32
    taps = {}
    for i in range(3):
        for q in range(2):
            rows = taps_in[i, q] * SMALL
            rows = [jnp.broadcast_to(rows[:, b : b + 1], (3, 128)) for b in range(3)]
            rows = jnp.where(third == 0, rows[0], jnp.where(third == 1, rows[1], jnp.where(third == 2, rows[2], 0.0)))
            for a in range(3):
                taps[i, q, a] = jnp.broadcast_to(rows[a : a + 1], (8, 128))

    planes = []
    for c in range(CAP):
        feats = []
        for i in range(3):
            base, row = rows_at(c, i)
            before = jnp.where(first_row, 0.0, pooled[pl.ds(base - 1, 32, stride=4), :])
            after = jnp.where(last_row, 0.0, pooled[pl.ds(base + 4, 32, stride=4), :])
            inside = row[1] + row[2]
            head = row[0] + inside
            window = (before + head, head + row[3], inside + row[3] + after)
            for q in range(2):
                mixed = sum(
                    (window[a].reshape(4, 8, 128) * taps[i, q, a][None]).reshape(32, 128) for a in range(3)
                )
                folded = mixed + pltpu.roll(mixed, 96, 1) + pltpu.roll(mixed, 64, 1)
                feats.append(folded.astype(jnp.bfloat16))
        planes.append(dot(jnp.concatenate(feats, axis=0), spread))

    for copy in copies:
        copy.wait()
    count = count_in[0, 0]
    total = jnp.zeros((8, 256), jnp.float32)
    for c in range(CAP):
        alive = jnp.where(c < count, 1.0, 0.0)
        part = jnp.zeros((8, 256), jnp.float32)
        for i in range(3):
            for q in range(2):
                at = (i * 2 + q) * 32
                part += fold(planes[c][at : at + 32] * rows_of(blocks[0, c], 3 * i + q))
            weight = None
            if c:
                weight = spans[0, c - 1] * rows_of(blocks[0, c - 1], 3 * i + 2)
            if c + 1 < CAP:
                span = jnp.where(c + 1 < count, spans[0, c + 1], 0.0)
                down = span * rows_of(blocks[0, c + 1], 3 * i + 2)
                weight = -down if weight is None else weight - down
            part += fold(normals[c][i * 32 : i * 32 + 32] * weight)
        total += alive * part
    out[0:8, :] = total


def send_kernel(part, partner, out):
    odd = lax.axis_index("core") == 1
    tile = partner[...]
    row = iota((8, 128), 0)

    def spread(at):
        return jnp.broadcast_to(tile[at : at + 1], (8, 128))

    span = jnp.where(odd, spread(2), -spread(0))
    block = jnp.where(odd, spread(3), spread(1)).astype(jnp.int32)
    weight = jnp.where(row == block, span, 0.0)
    near = part[16:24, :] * jnp.concatenate([weight, weight], axis=1)
    coef = jnp.sum(part[0:8, :] + near, axis=0, keepdims=True)
    coef = jnp.broadcast_to(coef, (8, 256))

    def pair(value):
        high = value.astype(jnp.bfloat16).astype(jnp.float32)
        return high, value - high

    high, low = pair(coef)
    wall, wall_low = pair(part[24:32, :128])
    wall = wall + pltpu.roll(wall_low, 64, 1)
    far, far_low = pair(jnp.where(odd, -spread(0), spread(2)))
    told = jnp.where(odd, spread(1), spread(3))
    picks = (high[:, :128], high[:, 128:], low[:, :128], low[:, 128:], wall, far, far_low, told)
    small = picks[-1]
    for at in range(7):
        small = jnp.where(row == at, picks[at], small)
    outer = part[8:16, :]
    whole = jnp.concatenate([outer[:, :128], outer[:, 128:], small], axis=0).astype(jnp.bfloat16)
    for copy_at in range(out.shape[0]):
        out[copy_at] = whole


def merge_kernel(rows, out, wide):
    odd = lax.axis_index("core") == 1
    chips = rows.shape[0] // SENT
    wide[...] = rows[...].astype(jnp.float32)

    def every(at):
        return wide[pl.ds(16 + at, chips, stride=SENT), :]

    low = jnp.sum(every(0) + every(2), axis=0, keepdims=True)
    high = jnp.sum(every(1) + every(3), axis=0, keepdims=True)
    wall = every(4)
    wall = wall + pltpu.roll(wall, 64, 1)
    sub = iota((8, 128), 0)
    reach = [jnp.zeros((8, 128), jnp.float32)] * 2
    order = ring(chips)
    for j in range(chips):
        at = SENT * order.index(j)
        span = wide[at + 21 : at + 22, :] + wide[at + 22 : at + 23, :]
        block = jnp.broadcast_to(wide[at + 23 : at + 24, :], (8, 128)).astype(jnp.int32)
        weight = jnp.where(sub == block, jnp.broadcast_to(span, (8, 128)), 0.0)
        before = wide[pl.ds(SENT * order.index(j - 1), 16), :] if j > 0 else jnp.zeros((16, 128), jnp.float32)
        after = wide[pl.ds(SENT * order.index(j + 1), 16), :] if j + 1 < chips else jnp.zeros((16, 128), jnp.float32)
        held = jnp.where(odd, before, after)
        reach = [reach[h] + weight * held[8 * h : 8 * h + 8] for h in range(2)]
    low = low + jnp.sum(reach[0], axis=0, keepdims=True)
    high = high + jnp.sum(reach[1], axis=0, keepdims=True)
    left = iota((8, 128), 1) < 64
    wide[0:chips, :] = wall
    wall = jnp.where(left, wide[pl.ds(0, 8, stride=2), :], wide[pl.ds(1, 8, stride=2), :])
    low = jnp.broadcast_to(low, (8, 128))
    high = jnp.broadcast_to(high, (8, 128))
    low_top = low.astype(jnp.bfloat16).astype(jnp.float32)
    high_top = high.astype(jnp.bfloat16).astype(jnp.float32)
    wall_top = wall.astype(jnp.bfloat16).astype(jnp.float32)
    small = jnp.where(sub == 0, low_top, jnp.where(sub == 1, high_top, jnp.where(sub == 2, low - low_top, jnp.where(sub == 3, high - high_top, 0.0))))
    whole = jnp.concatenate([wall_top, wall - wall_top, small], axis=0).astype(jnp.bfloat16)
    for copy_at in range(out.shape[0]):
        out[copy_at] = whole


def finish_kernel(rows, sketch, gram, wide):
    wide[...] = rows[...].astype(jnp.float32)

    def across(core, at):
        return wide[pl.ds(16 * SENT * core + at, 16, stride=SENT), :]

    def both(at):
        return across(0, at) + across(0, at + 2) + across(1, at) + across(1, at + 2)

    coef = jnp.concatenate([both(16), both(17)], axis=1)
    coef_high, coef_low = split(coef)
    walls = [
        jnp.concatenate([across(core, r), across(core, r + 8)], axis=0).astype(jnp.bfloat16)
        for core in range(2)
        for r in range(8)
    ]
    wall = jnp.concatenate(walls, axis=1)
    product = lax.dot_general(wall, wall, (((1,), (1,)), ((), ())), preferred_element_type=jnp.float32)
    product = product[0:16] + product[16:32]
    inner = product[:, 0:16] + product[:, 16:32]
    inner_high, inner_low = split(inner)
    right = dot(inner_high, coef_high) + dot(inner_low, coef_high) + dot(inner_high, coef_low)
    right_high, right_low = split(right * (1.0 / 2048.0))
    left = jnp.concatenate([coef_high, coef_low, coef_high], axis=0)
    gram[...] = lax.dot_general(
        left,
        jnp.concatenate([right_high, right_high, right_low], axis=0),
        OVER_ROWS,
        preferred_element_type=jnp.float32,
    )
    core, chip, snap = lax.axis_index("core"), lax.axis_index("z"), lax.axis_index("snap")
    place = lax.rem(chip * pow(STEP, -1, 16), 16)
    row_at = core * 8 + lax.shift_right_logical(place, 1)
    mine = jnp.zeros((16, 128), jnp.float32)
    for c in range(2):
        for r in range(8):
            mine = jnp.where(row_at == c * 8 + r, across(c, r) + across(c, r + 8), mine)
    target = iota((16, 128), 1) - (place & 1) * 64 - 2 * snap
    for m in range(2):
        for x in range(2):
            column = jnp.sum(jnp.where(target == 32 * m + x, mine, 0.0), axis=1, keepdims=True)
            sketch[m, 0, x : x + 1, :] = jnp.sum(column * coef, axis=0, keepdims=True)


def per_device(velocity, plane_count, inv_span, kernels, omega_block, omega_table, omega_stream, wall_shear):
    f32, bf16 = jnp.float32, jnp.bfloat16
    chips, snaps = lax.axis_size("z"), lax.axis_size("snap")
    count = jnp.broadcast_to(plane_count.reshape(1, 1), (1, 128))
    tile = jax.ShapeDtypeStruct((8, 128), f32)
    base = call(blank_kernel, "blank", tile, [], cost=LONG)()
    own = call(pack_kernel, "pack", tile, [VMEM] * 4, cost=LONG)(
        count, inv_span, omega_block, base
    )
    partner = lax.ppermute(own, "core", [(0, 1), (1, 0)])
    part = call(
        project_kernel,
        "project",
        jax.ShapeDtypeStruct((32, 256), f32),
        [VMEM] * 8,
        [
            pltpu.VMEM((ROWS + 2 * PAD, 128), f32),
            pltpu.SMEM((1, 128), jnp.int32),
            pltpu.SMEM((1, CAP), f32),
            pltpu.SMEM((1, CAP), jnp.int32),
            pltpu.SemaphoreType.DMA((3,)),
        ],
        cost=LONG,
        params=SPREAD,
    )(
        count,
        inv_span,
        omega_block,
        kernels,
        velocity.reshape(ROWS, 128),
        omega_table.reshape(BLOCKS, 288, 256),
        omega_stream,
        wall_shear.reshape(8, 128),
    )
    sent = call(send_kernel, "send", jax.ShapeDtypeStruct((chips, SENT, 128), bf16), [VMEM] * 2)(
        part, partner
    )
    got = lax.all_to_all(sent, "z", 0, 0, tiled=True, axis_index_groups=[ring(chips)]).reshape(chips * SENT, 128)
    sent = call(
        merge_kernel,
        "merge",
        jax.ShapeDtypeStruct((snaps * 2, SENT, 128), bf16),
        [VMEM],
        [pltpu.VMEM((chips * SENT, 128), f32)],
    )(got)
    got = lax.all_to_all(sent, ("core", "snap"), 0, 0, tiled=True).reshape(snaps * 2 * SENT, 128)
    return call(
        finish_kernel,
        "finish",
        (jax.ShapeDtypeStruct((2, 1, 2, 256), f32), jax.ShapeDtypeStruct((256, 256), f32)),
        [VMEM],
        [pltpu.VMEM((snaps * 2 * SENT, 128), f32)],
    )(got)


def solution(mesh):
    chips = mesh.shape["plane"] // 2
    fine = Mesh(mesh.devices.reshape(mesh.shape["snap"], chips, 2), ("snap", "z", "core"))
    plane = ("z", "core")
    return jax.shard_map(
        per_device,
        mesh=fine,
        in_specs=(
            P("snap", plane, None, None, None),
            P(plane),
            P(plane, None),
            P(),
            P(plane, None),
            P(),
            P(),
            P("snap", None, plane, None),
        ),
        out_specs=(P(None, plane, "snap", None), P()),
        check_vma=False,
    )
```

```python
import jax
import jax.numpy as jnp
from jax import lax
from jax.experimental import pallas as pl
from jax.experimental.pallas import tpu as pltpu
from jax.sharding import Mesh, PartitionSpec as P

CAP = 4
BLOCKS = 8
ROWS = 1536
PAD = 8
SENT = 24
STEP = 13
SMALL = 1.0 / 16.0
LONG = pl.CostEstimate(flops=10**10, bytes_accessed=10**7, transcendentals=0)
GRANT = pltpu.CompilerParams(vmem_limit_bytes=8 << 20)
SPREAD = pltpu.CompilerParams(vmem_limit_bytes=8 << 20)
VMEM = pl.BlockSpec(memory_space=pltpu.VMEM)
OVER_ROWS = (((0,), (0,)), ((), ()))


def iota(shape, dim):
    return lax.broadcasted_iota(jnp.int32, shape, dim)


def ring(chips):
    return [STEP * place % chips for place in range(chips)]


def split(value):
    high = value.astype(jnp.bfloat16)
    low = (value - high.astype(jnp.float32)).astype(jnp.bfloat16)
    return high, low


def dot(left, right):
    return jnp.dot(left, right, preferred_element_type=jnp.float32)


def call(kernel, name, out, ins, scratch=(), cost=None, params=GRANT):
    return pl.pallas_call(
        kernel,
        out_shape=out,
        in_specs=ins,
        out_specs=jax.tree.map(lambda _: VMEM, out),
        scratch_shapes=list(scratch),
        compiler_params=params,
        cost_estimate=cost,
        name=name,
    )


def blank_kernel(out):
    out[...] = jnp.zeros((8, 128), jnp.float32)


def pack_kernel(count, spans, blocks, base, out):
    row = iota((8, 128), 0)
    last = iota((1, CAP), 1) == count[:, 0:CAP] - 1
    marks = blocks[...].astype(jnp.float32)
    tile = base[...]
    for at, values in ((0, spans[...]), (1, marks)):
        final = jnp.sum(jnp.where(last, values, 0.0), axis=1, keepdims=True)
        tile = jnp.where(row == at, jnp.broadcast_to(values[:, 0:1], (8, 128)), tile)
        tile = jnp.where(row == at + 2, jnp.broadcast_to(final, (8, 128)), tile)
    out[...] = tile


def project_kernel(
    count_vec, spans_vec, blocks_vec, taps_in, vel, table, stream, shear, out, pooled, count_in, spans, blocks, sems
):
    pairs = ((count_vec, count_in), (spans_vec, spans), (blocks_vec, blocks))
    copies = [pltpu.make_async_copy(source, target, sems.at[at]) for at, (source, target) in enumerate(pairs)]
    for copy in copies:
        copy.start()
    odd = lax.axis_index("core") == 1

    lane = iota((128, 128), 1)
    gap = iota((128, 128), 0) - 4 * (lane % 32) - lane // 32 + 1
    pool = jnp.where((gap >= 0) & (gap < 4) & (lane < 96), 1.0, 0.0).astype(jnp.bfloat16)
    group = iota((8, 128), 1) // 32

    zeros = jnp.zeros((32, 256), jnp.bfloat16)
    omega = stream[...]
    spread = jnp.concatenate([omega, zeros, zeros, zeros], axis=0)
    centre = jnp.concatenate([zeros, omega, zeros, zeros] * 2, axis=0)
    first_row = iota((32, 128), 0) == 0
    last_row = iota((32, 128), 0) == 31

    for c in range(CAP):
        pooled[pl.ds(PAD + c * 384, 384), :] = dot(vel[pl.ds(c * 384, 384), :], pool)

    def rows_at(c, i):
        base = PAD + (c * 3 + i) * 128
        return base, [pooled[pl.ds(base + j, 32, stride=4), :] for j in range(4)]

    normals = []
    for c in range(CAP):
        centres = []
        for i in range(3):
            row = rows_at(c, i)[1]
            centres.append(jnp.concatenate(split((row[0] + row[1] + row[2] + row[3]) * SMALL), axis=1))
        normals.append(dot(jnp.concatenate(centres, axis=0), centre))

    def rows_of(block, channel):
        return table[block, channel * 32 : channel * 32 + 32, :].astype(jnp.float32)

    def fold(value):
        return value.reshape(4, 8, 256).sum(0)

    counts = jnp.concatenate([count_vec[...], count_vec[...]], axis=1)
    final = sum(jnp.where(counts == c + 1, 1.0, 0.0) * normals[c] for c in range(CAP))
    edges = (jnp.where(odd, final, normals[0]), jnp.where(odd, normals[0], final))
    found = ([], [])
    for block in range(BLOCKS):
        parts = [jnp.zeros((8, 256), jnp.float32)] * 2
        for i in range(3):
            rows = rows_of(block, 3 * i + 2)
            parts = [part + fold(edge[i * 32 : i * 32 + 32] * rows) for part, edge in zip(parts, edges)]
        for part, rows in zip(parts, found):
            rows.append(jnp.sum(part, axis=0, keepdims=True))
    out[8:16, :] = jnp.concatenate(found[0], axis=0)
    out[16:24, :] = jnp.concatenate(found[1], axis=0)

    wall = dot(shear[...], pool) * SMALL
    first = jnp.broadcast_to(jnp.sum(wall[0:4], axis=0, keepdims=True), (8, 128))
    second = jnp.broadcast_to(jnp.sum(wall[4:8], axis=0, keepdims=True), (8, 128))
    low = jnp.where(group == 0, pltpu.roll(first, 96, 1), jnp.where(group == 1, second, 0.0))
    out[24:32, :] = jnp.concatenate([low, low], axis=1)


    third = iota((3, 128), 1) // 32
    taps = {}
    for i in range(3):
        for q in range(2):
            rows = taps_in[i, q] * SMALL
            rows = [jnp.broadcast_to(rows[:, b : b + 1], (3, 128)) for b in range(3)]
            rows = jnp.where(third == 0, rows[0], jnp.where(third == 1, rows[1], jnp.where(third == 2, rows[2], 0.0)))
            for a in range(3):
                taps[i, q, a] = jnp.broadcast_to(rows[a : a + 1], (8, 128))

    planes = []
    for c in range(CAP):
        feats = []
        for i in range(3):
            base, row = rows_at(c, i)
            before = jnp.where(first_row, 0.0, pooled[pl.ds(base - 1, 32, stride=4), :])
            after = jnp.where(last_row, 0.0, pooled[pl.ds(base + 4, 32, stride=4), :])
            inside = row[1] + row[2]
            head = row[0] + inside
            window = (before + head, head + row[3], inside + row[3] + after)
            for q in range(2):
                mixed = sum(
                    (window[a].reshape(4, 8, 128) * taps[i, q, a][None]).reshape(32, 128) for a in range(3)
                )
                folded = mixed + pltpu.roll(mixed, 96, 1) + pltpu.roll(mixed, 64, 1)
                feats.append(folded.astype(jnp.bfloat16))
        planes.append(dot(jnp.concatenate(feats, axis=0), spread))

    for copy in copies:
        copy.wait()
    count = count_in[0, 0]
    total = jnp.zeros((8, 256), jnp.float32)
    for c in range(CAP):
        alive = jnp.where(c < count, 1.0, 0.0)
        part = jnp.zeros((8, 256), jnp.float32)
        for i in range(3):
            for q in range(2):
                at = (i * 2 + q) * 32
                part += fold(planes[c][at : at + 32] * rows_of(blocks[0, c], 3 * i + q))
            weight = None
            if c:
                weight = spans[0, c - 1] * rows_of(blocks[0, c - 1], 3 * i + 2)
            if c + 1 < CAP:
                span = jnp.where(c + 1 < count, spans[0, c + 1], 0.0)
                down = span * rows_of(blocks[0, c + 1], 3 * i + 2)
                weight = -down if weight is None else weight - down
            part += fold(normals[c][i * 32 : i * 32 + 32] * weight)
        total += alive * part
    out[0:8, :] = total


def send_kernel(part, partner, out):
    odd = lax.axis_index("core") == 1
    tile = partner[...]
    row = iota((8, 128), 0)

    def spread(at):
        return jnp.broadcast_to(tile[at : at + 1], (8, 128))

    span = jnp.where(odd, spread(2), -spread(0))
    block = jnp.where(odd, spread(3), spread(1)).astype(jnp.int32)
    weight = jnp.where(row == block, span, 0.0)
    near = part[16:24, :] * jnp.concatenate([weight, weight], axis=1)
    coef = jnp.sum(part[0:8, :] + near, axis=0, keepdims=True)
    coef = jnp.broadcast_to(coef, (8, 256))

    def pair(value):
        high = value.astype(jnp.bfloat16).astype(jnp.float32)
        return high, value - high

    high, low = pair(coef)
    wall, wall_low = pair(part[24:32, :128])
    wall = wall + pltpu.roll(wall_low, 64, 1)
    far, far_low = pair(jnp.where(odd, -spread(0), spread(2)))
    told = jnp.where(odd, spread(1), spread(3))
    picks = (high[:, :128], high[:, 128:], low[:, :128], low[:, 128:], wall, far, far_low, told)
    small = picks[-1]
    for at in range(7):
        small = jnp.where(row == at, picks[at], small)
    outer = part[8:16, :]
    whole = jnp.concatenate([outer[:, :128], outer[:, 128:], small], axis=0).astype(jnp.bfloat16)
    for copy_at in range(out.shape[0]):
        out[copy_at] = whole


def merge_kernel(rows, out, wide):
    odd = lax.axis_index("core") == 1
    chips = rows.shape[0] // SENT
    wide[...] = rows[...].astype(jnp.float32)

    def every(at):
        return wide[pl.ds(16 + at, chips, stride=SENT), :]

    low = jnp.sum(every(0) + every(2), axis=0, keepdims=True)
    high = jnp.sum(every(1) + every(3), axis=0, keepdims=True)
    wall = every(4)
    wall = wall + pltpu.roll(wall, 64, 1)
    sub = iota((8, 128), 0)
    reach = [jnp.zeros((8, 128), jnp.float32)] * 2
    order = ring(chips)
    for j in range(chips):
        at = SENT * order.index(j)
        span = wide[at + 21 : at + 22, :] + wide[at + 22 : at + 23, :]
        block = jnp.broadcast_to(wide[at + 23 : at + 24, :], (8, 128)).astype(jnp.int32)
        weight = jnp.where(sub == block, jnp.broadcast_to(span, (8, 128)), 0.0)
        before = wide[pl.ds(SENT * order.index(j - 1), 16), :] if j > 0 else jnp.zeros((16, 128), jnp.float32)
        after = wide[pl.ds(SENT * order.index(j + 1), 16), :] if j + 1 < chips else jnp.zeros((16, 128), jnp.float32)
        held = jnp.where(odd, before, after)
        reach = [reach[h] + weight * held[8 * h : 8 * h + 8] for h in range(2)]
    low = low + jnp.sum(reach[0], axis=0, keepdims=True)
    high = high + jnp.sum(reach[1], axis=0, keepdims=True)
    left = iota((8, 128), 1) < 64
    wide[0:chips, :] = wall
    wall = jnp.where(left, wide[pl.ds(0, 8, stride=2), :], wide[pl.ds(1, 8, stride=2), :])
    low = jnp.broadcast_to(low, (8, 128))
    high = jnp.broadcast_to(high, (8, 128))
    low_top = low.astype(jnp.bfloat16).astype(jnp.float32)
    high_top = high.astype(jnp.bfloat16).astype(jnp.float32)
    wall_top = wall.astype(jnp.bfloat16).astype(jnp.float32)
    small = jnp.where(sub == 0, low_top, jnp.where(sub == 1, high_top, jnp.where(sub == 2, low - low_top, jnp.where(sub == 3, high - high_top, 0.0))))
    whole = jnp.concatenate([wall_top, wall - wall_top, small], axis=0).astype(jnp.bfloat16)
    for copy_at in range(out.shape[0]):
        out[copy_at] = whole


def finish_kernel(rows, sketch, gram, wide):
    wide[...] = rows[...].astype(jnp.float32)

    def across(core, at):
        return wide[pl.ds(SENT * core + at, 16, stride=2 * SENT), :]

    def both(at):
        return across(0, at) + across(0, at + 2) + across(1, at) + across(1, at + 2)

    coef = jnp.concatenate([both(16), both(17)], axis=1)
    coef_high, coef_low = split(coef)
    walls = [
        jnp.concatenate([across(core, r), across(core, r + 8)], axis=0).astype(jnp.bfloat16)
        for core in range(2)
        for r in range(8)
    ]
    wall = jnp.concatenate(walls, axis=1)
    product = lax.dot_general(wall, wall, (((1,), (1,)), ((), ())), preferred_element_type=jnp.float32)
    product = product[0:16] + product[16:32]
    inner = product[:, 0:16] + product[:, 16:32]
    inner_high, inner_low = split(inner)
    right = dot(inner_high, coef_high) + dot(inner_low, coef_high) + dot(inner_high, coef_low)
    right_high, right_low = split(right * (1.0 / 2048.0))
    left = jnp.concatenate([coef_high, coef_low, coef_high], axis=0)
    gram[...] = lax.dot_general(
        left,
        jnp.concatenate([right_high, right_high, right_low], axis=0),
        OVER_ROWS,
        preferred_element_type=jnp.float32,
    )
    core, chip, snap = lax.axis_index("core"), lax.axis_index("z"), lax.axis_index("snap")
    place = lax.rem(chip * pow(STEP, -1, 16), 16)
    row_at = core * 8 + lax.shift_right_logical(place, 1)
    mine = jnp.zeros((16, 128), jnp.float32)
    for c in range(2):
        for r in range(8):
            mine = jnp.where(row_at == c * 8 + r, across(c, r) + across(c, r + 8), mine)
    target = iota((16, 128), 1) - (place & 1) * 64 - 2 * snap
    for m in range(2):
        for x in range(2):
            column = jnp.sum(jnp.where(target == 32 * m + x, mine, 0.0), axis=1, keepdims=True)
            sketch[m, 0, x : x + 1, :] = jnp.sum(column * coef, axis=0, keepdims=True)


def per_device(velocity, plane_count, inv_span, kernels, omega_block, omega_table, omega_stream, wall_shear):
    f32, bf16 = jnp.float32, jnp.bfloat16
    chips, snaps = lax.axis_size("z"), lax.axis_size("snap")
    count = jnp.broadcast_to(plane_count.reshape(1, 1), (1, 128))
    tile = jax.ShapeDtypeStruct((8, 128), f32)
    base = call(blank_kernel, "blank", tile, [], cost=LONG)()
    own = call(pack_kernel, "pack", tile, [VMEM] * 4, cost=LONG)(
        count, inv_span, omega_block, base
    )
    partner = lax.ppermute(own, "core", [(0, 1), (1, 0)])
    part = call(
        project_kernel,
        "project",
        jax.ShapeDtypeStruct((32, 256), f32),
        [VMEM] * 8,
        [
            pltpu.VMEM((ROWS + 2 * PAD, 128), f32),
            pltpu.SMEM((1, 128), jnp.int32),
            pltpu.SMEM((1, CAP), f32),
            pltpu.SMEM((1, CAP), jnp.int32),
            pltpu.SemaphoreType.DMA((3,)),
        ],
        cost=LONG,
        params=SPREAD,
    )(
        count,
        inv_span,
        omega_block,
        kernels,
        velocity.reshape(ROWS, 128),
        omega_table.reshape(BLOCKS, 288, 256),
        omega_stream,
        wall_shear.reshape(8, 128),
    )
    sent = call(send_kernel, "send", jax.ShapeDtypeStruct((chips, SENT, 128), bf16), [VMEM] * 2)(
        part, partner
    )
    got = lax.all_to_all(sent, "z", 0, 0, tiled=True, axis_index_groups=[ring(chips)]).reshape(chips * SENT, 128)
    sent = call(
        merge_kernel,
        "merge",
        jax.ShapeDtypeStruct((snaps * 2, SENT, 128), bf16),
        [VMEM],
        [pltpu.VMEM((chips * SENT, 128), f32)],
    )(got)
    got = lax.all_to_all(sent, ("snap", "core"), 0, 0, tiled=True).reshape(snaps * 2 * SENT, 128)
    return call(
        finish_kernel,
        "finish",
        (jax.ShapeDtypeStruct((2, 1, 2, 256), f32), jax.ShapeDtypeStruct((256, 256), f32)),
        [VMEM],
        [pltpu.VMEM((snaps * 2 * SENT, 128), f32)],
    )(got)


def solution(mesh):
    chips = mesh.shape["plane"] // 2
    fine = Mesh(mesh.devices.reshape(mesh.shape["snap"], chips, 2), ("snap", "z", "core"))
    plane = ("z", "core")
    return jax.shard_map(
        per_device,
        mesh=fine,
        in_specs=(
            P("snap", plane, None, None, None),
            P(plane),
            P(plane, None),
            P(),
            P(plane, None),
            P(),
            P(),
            P("snap", None, plane, None),
        ),
        out_specs=(P(None, plane, "snap", None), P()),
        check_vma=False,
    )
```
